128 devices in a mesh: gx: 8 (over x, core), bulk: 16 (over y, z).
Axes of the slice: x: 4, y: 4, z: 4, core: 2. Of those that a mesh axis runs over, the one named last changes fastest.
Arguments:
- basis: bfloat16 [8, 64, 524288], P(None, None, ('gx', 'bulk')), may hold values from -6 to 6
- near_blocks: bfloat16 [2048, 8, 256, 256], P(('gx', 'bulk')), may hold values from -0.125 to 0.125
- near_src: int32 [2048, 8], P(('gx', 'bulk')), may hold values from 0 to 47
- near_count: int32 [2048], P(('gx', 'bulk')), may hold values from 1 to 8
- p2m: bfloat16 [2048, 256, 128], P(('gx', 'bulk')), may hold values from -0.375 to 0.375
- m2l: bfloat16 [16, 128, 128], replicated, may hold values from -0.25 to 0.25
- send_list: int32 [128, 128, 4], P(('gx', 'bulk')), may hold values from 0 to 15
- send_count: int32 [128, 128], P(('gx', 'bulk')), may hold values from 0 to 4
- far_src: int32 [2048, 32], P(('gx', 'bulk')), may hold values from 0 to 511
- far_class: int32 [2048, 32], P(('gx', 'bulk')), may hold values from 0 to 15
Outputs:
- next_block: bfloat16 [64, 524288], P(None, ('gx', 'bulk'))
- projections: float32 [8, 64, 64], replicated
- factor: float32 [64, 64], replicated
The draws below stay inside these ranges and needn't reach their ends.
All inputs are finite; a program needn't handle non-finite values.
Results may differ from the reference program's by a relative error of at most 0.012.
Values may be sent and summed in bfloat16 or wider, within the bound.
A program may use at most 128 MiB of HBM per device.

```python
import jax
import jax.numpy as jnp
from jax import lax

P_SIZE = 256
RHS = 64
Q = 128
KB = 8
CLS = 16
NB = 8
FL = 32
SLOT = 4
LDEV = 16
LEAVES = 2048
ROWS = 524288
N_GX = 8
N_BULK = 16


def plant(result, rng, least, top_value):
    shape = result.shape
    place = [jax.random.randint(jax.random.fold_in(rng, axis), (), 0, shape[axis]) for axis in range(len(shape))]
    result = result.at[tuple(place)].set(least)
    longest = shape.index(max(shape))
    place[longest] = (place[longest] + 1) % shape[longest]
    return result.at[tuple(place)].set(top_value)


def levels(rng, shape, split, low, high):
    def one(position, shards_of):
        heights = jax.random.uniform(jax.random.fold_in(jax.random.fold_in(rng, 6), position), (shards_of,), jnp.float32, low / len(split), high / len(split))
        return jnp.repeat(jnp.exp(heights), shape[position] // shards_of).reshape((-1,) + (1,) * (len(shape) - position - 1))

    gain = one(*split[0])
    for cut in split[1:]:
        gain = gain * one(*cut)
    return gain


def centred(own_key, extent, spread, most, shards=(), held_as=jnp.bfloat16):
    array = jax.random.normal(own_key, extent, jnp.float32) * spread
    if len(shards) > 0:
        array = levels(own_key, extent, shards, -0.22, 0.18) * array
    return jnp.clip(array, min=-most, max=most).astype(held_as)


def setup_inputs(seed: int = 0) -> dict:
    splits = jax.random.split(jax.random.key(seed), 11)
    basis = centred(splits[0], (KB, RHS, ROWS), 1.0, 6.0, ((2, 128),))
    near_blocks = centred(splits[1], (LEAVES, NB, P_SIZE, P_SIZE), (P_SIZE * NB) ** -0.5, 0.125, ((0, 128),))
    near_src = plant(jax.random.randint(splits[2], (LEAVES, NB), 0, 3 * LDEV), jax.random.fold_in(splits[2], 1), 0, (3 * LDEV) - 1).astype(jnp.int32)
    near_count = plant(jax.random.randint(splits[3], (LEAVES,), 1, NB + 1), jax.random.fold_in(splits[3], 1), 1, NB).astype(jnp.int32)
    p2m = centred(splits[4], (LEAVES, P_SIZE, Q), P_SIZE ** -0.5, 0.375, ((0, 128),))
    m2l = centred(splits[5], (CLS, Q, Q), (4 * Q) ** -0.5, 0.25)
    send_list = plant(jax.random.randint(splits[6], (N_GX * N_BULK, N_GX * N_BULK, SLOT), 0, LDEV), jax.random.fold_in(splits[6], 1), 0, LDEV - 1).astype(jnp.int32)
    send_count = plant(jax.random.randint(splits[7], (N_GX * N_BULK, N_GX * N_BULK), 0, SLOT + 1), jax.random.fold_in(splits[7], 1), 0, SLOT).astype(jnp.int32)
    far_src = plant(jax.random.randint(splits[8], (LEAVES, FL), 0, N_GX * N_BULK * SLOT), jax.random.fold_in(splits[8], 1), 0, (N_GX * N_BULK * SLOT) - 1).astype(jnp.int32)
    far_class = plant(jax.random.randint(splits[9], (LEAVES, FL), 0, CLS), jax.random.fold_in(splits[9], 1), 0, CLS - 1).astype(jnp.int32)
    return dict(basis=basis, near_blocks=near_blocks, near_src=near_src, near_count=near_count, p2m=p2m, m2l=m2l, send_list=send_list, send_count=send_count, far_src=far_src, far_class=far_class)


def reference(basis, near_blocks, near_src, near_count, p2m, m2l, send_list, send_count, far_src, far_class):
    ndev = N_GX * N_BULK
    x = basis[KB - 1].reshape(RHS, ndev, LDEV, P_SIZE)
    xpad = jnp.pad(x, ((0, 0), (N_BULK, N_BULK), (0, 0), (0, 0)))
    blocks_dev = near_blocks.reshape(ndev, LDEV, NB, P_SIZE, P_SIZE)
    nsrc_dev = near_src.reshape(ndev, LDEV, NB)
    ncount_dev = near_count.reshape(ndev, LDEV)
    p2m_dev = p2m.reshape(ndev, LDEV, P_SIZE, Q)
    fsrc_dev = far_src.reshape(ndev, LDEV, FL)
    fcls_dev = far_class.reshape(ndev, LDEV, FL)

    def multipoles(dev):
        return jnp.einsum('rlp,lpq->lrq', x[:, dev].astype(jnp.float32), p2m_dev[dev].astype(jnp.float32)).astype(jnp.bfloat16)
    mult = lax.map(multipoles, jnp.arange(ndev, dtype=jnp.int32))

    def per_device(dev):
        window = lax.dynamic_slice_in_dim(xpad, dev, 2 * N_BULK + 1, 1)
        three = jnp.concatenate([window[:, 0], window[:, N_BULK], window[:, 2 * N_BULK]], axis=1)
        picked = jnp.take(three, nsrc_dev[dev].reshape(-1), axis=1).reshape(RHS, LDEV, NB, P_SIZE)
        live = (jnp.arange(NB, dtype=jnp.int32)[None, :] < ncount_dev[dev][:, None]).astype(jnp.float32)
        picked = picked.astype(jnp.float32) * live[None, :, :, None]
        near = jnp.einsum('rlkq,lkpq->rlp', picked, blocks_dev[dev].astype(jnp.float32))
        sender = fsrc_dev[dev] // SLOT
        slot = fsrc_dev[dev] % SLOT
        leaf = send_list[sender, dev, slot]
        valid = (slot < send_count[sender, dev]).astype(jnp.float32)
        sources = mult[sender, leaf].astype(jnp.float32) * valid[:, :, None, None]
        onehot = (fcls_dev[dev][:, :, None] == jnp.arange(CLS, dtype=jnp.int32)[None, None, :]).astype(jnp.float32)
        gathered = jnp.einsum('lec,lerq->clrq', onehot, sources).astype(jnp.bfloat16)
        local = jnp.einsum('clrq,cqs->lrs', gathered.astype(jnp.float32), m2l.astype(jnp.float32)).astype(jnp.bfloat16)
        far = jnp.einsum('lrq,lpq->rlp', local.astype(jnp.float32), p2m_dev[dev].astype(jnp.float32))
        return x[:, dev].astype(jnp.float32) + near + far
    image = lax.map(per_device, jnp.arange(ndev, dtype=jnp.int32))
    image = jnp.transpose(image, (1, 0, 2, 3)).reshape(RHS, ROWS)
    vecs = basis.astype(jnp.float32)
    hi = lax.Precision.HIGHEST
    projections = jnp.einsum('krn,sn->krs', vecs, image, precision=hi) / ROWS
    resid = image - jnp.einsum('krs,krn->sn', projections, vecs, precision=hi)
    gram = jnp.dot(resid, resid.T, precision=hi) / ROWS
    factor = jnp.linalg.cholesky(gram)
    next_block = lax.linalg.triangular_solve(factor, resid, left_side=True, lower=True).astype(jnp.bfloat16)
    return (next_block, projections, factor)
```

```python
import functools

import jax
import jax.numpy as jnp
from jax import lax
from jax.experimental import pallas as pl
from jax.experimental.pallas import tpu as pltpu
from jax.sharding import Mesh
from jax.sharding import PartitionSpec as P

ALL = ("x", "c", "y", "z")
ORDERS = (("x", "y", "z"), ("y", "z", "x"), ("z", "x", "y"))
MESH = pl.DeviceIdType.MESH
F32, BF16 = jnp.float32, jnp.bfloat16
LIMIT = 67043328
EXTRA = 16
NT = (((1,), (1,)), ((), ()))
TN = (((0,), (0,)), ((), ()))


def dot(a, b, dims=(((1,), (0,)), ((), ()))):
    return lax.dot_general(a, b, dims, preferred_element_type=F32)


def halves(values):
    upper = values.astype(BF16)
    return upper, (values - upper.astype(F32)).astype(BF16)


def mult_kernel(per_step, rhs, x_ref, p_ref, list_ref, count_ref, out_ref, leaf_ref):
    step = pl.program_id(0)
    panels = p_ref.shape[1]
    for i in range(per_step):
        vector = x_ref[0, :, i * panels : (i + 1) * panels]
        leaf_ref[i] = vector
        block = dot(vector, p_ref[i]).astype(BF16)
        at = pl.multiple_of((step * per_step + i) * rhs, rhs)
        out_ref[pl.ds(at, rhs), :] = block

    @pl.when(step == 0)
    def _():
        peers, slots = list_ref.shape[1:]
        widen = (
            lax.broadcasted_iota(jnp.int32, (slots, EXTRA), 0)
            == lax.broadcasted_iota(jnp.int32, (slots, EXTRA), 1)
        ).astype(BF16)
        eye = (
            lax.broadcasted_iota(jnp.int32, (peers, peers), 0)
            == lax.broadcasted_iota(jnp.int32, (peers, peers), 1)
        ).astype(BF16)
        wide = dot(list_ref[0].astype(F32).astype(BF16), widen).astype(BF16)
        table = dot(wide, eye, TN)
        counts = jnp.broadcast_to(count_ref[...].astype(F32), (EXTRA, peers))
        row = lax.broadcasted_iota(jnp.int32, (EXTRA, peers), 0)
        rows = out_ref.shape[0]
        out_ref[rows - EXTRA : rows, :] = jnp.where(row == slots, counts, table).astype(BF16)


def multipoles(basis, p2m, send_list, send_count):
    blocks, rhs, columns = basis.shape
    leaves, panels, terms = p2m.shape
    steps = 4
    per = leaves // steps
    rows = leaves * rhs + EXTRA
    return pl.pallas_call(
        functools.partial(mult_kernel, per, rhs),
        grid=(steps,),
        in_specs=[
            pl.BlockSpec((1, rhs, per * panels), lambda i: (blocks - 1, 0, i)),
            pl.BlockSpec((per, panels, terms), lambda i: (i, 0, 0)),
            pl.BlockSpec(send_list.shape, lambda i: (0, 0, 0)),
            pl.BlockSpec(send_count.shape, lambda i: (0, 0)),
        ],
        out_specs=(
            pl.BlockSpec((rows, terms), lambda i: (0, 0)),
            pl.BlockSpec((per, rhs, panels), lambda i: (i, 0, 0)),
        ),
        out_shape=(
            jax.ShapeDtypeStruct((rows, terms), BF16),
            jax.ShapeDtypeStruct((leaves, rhs, panels), BF16),
        ),
        name="multipoles",
    )(basis, p2m, send_list, send_count)


def spread_kernel(
    cuts, mult_ref, x_ref, near_blocks_ref, src_ref, live_ref,
    all_ref, base_ref,
    xbuf, nbuf, send_sem, recv_sem, sib_send, sib_recv, halo_send, halo_recv, own_sem, x_sem, nsem,
):
    me = {name: lax.axis_index(name) for name in ALL}
    leaves = near_blocks_ref.shape[0]
    slots = near_blocks_ref.shape[1]
    panels = near_blocks_ref.shape[2]
    depth = nbuf.shape[0]
    column = me["x"] * 2 + me["c"]

    def at(axis, by):
        return lax.rem(me[axis] + (by + 4), 4)

    def near_copy(leaf, slot):
        return pltpu.make_async_copy(near_blocks_ref.at[leaf], nbuf.at[slot], nsem.at[slot])

    own_x = pltpu.make_async_copy(x_ref, xbuf.at[pl.ds(leaves, leaves)], x_sem)
    own_x.start()
    for leaf in range(depth):
        near_copy(leaf, leaf).start()

    other = {"c": 1 - me["c"]}
    barrier = pltpu.get_barrier_semaphore()
    peers = [{axis: at(axis, by)} for axis in ("x", "y", "z") for by in (1, -1)]
    peers.append(other)
    gx = 8
    after_col = lax.rem(column + 1, gx)
    before_col = lax.rem(column + gx - 1, gx)
    after = {"x": after_col // 2, "c": lax.rem(after_col, 2)}
    before = {"x": before_col // 2, "c": lax.rem(before_col, 2)}
    peers += [after, before]
    for peer in peers:
        pl.semaphore_signal(barrier, inc=1, device_id=peer, device_id_type=MESH)
    pl.semaphore_wait(barrier, len(peers))

    def place(where, rows, core):
        index = []
        for name in ALL:
            if name == "c":
                index.append(core)
            elif name in where:
                index.append(where[name])
            else:
                index.append(slice(None))
        return all_ref.at[tuple(index) + (pl.ds(rows[0], rows[1] - rows[0]),)]

    units = [(0, None, None)]
    units += [(1, r, None) for r in (0, -1, 1, 2)]
    units += [(2, r, 0) for r in (0, -1, 1, 2)]
    units += [(2, None, r) for r in (-1, 1, 2)]
    number = {u: i for i, u in enumerate(units)}
    started = []

    def where_of(colour, unit, by):
        axes = ORDERS[colour]
        phase, first, second = unit
        where = {}
        if phase == 0:
            where = {axes[0]: by, axes[1]: 0, axes[2]: 0}
        elif phase == 1:
            where = {axes[0]: first, axes[1]: by, axes[2]: 0}
        else:
            where = {axes[1]: second, axes[2]: by}
            if first is not None:
                where[axes[0]] = first
        return where

    def rows_of(colour, part):
        low, high = cuts[colour], cuts[colour + 1]
        middle = low + (high - low) // 32 * 16
        return {"all": (low, high), "lower": (low, middle), "upper": (middle, high)}[part]

    def remote(colour, unit, kind):
        axis = ORDERS[colour][unit[0]]
        by, to, part = ((0, 1, "all"), (0, -1, "all"), (-1, 1, "lower"), (1, -1, "upper"))[kind]
        offsets = where_of(colour, unit, by)
        where = {name: at(name, v) for name, v in offsets.items()}
        rows = rows_of(colour, part)
        dst = place(where, rows, me["c"])
        src = dst
        if len(offsets) == 3 and all(v == 0 for v in offsets.values()):
            src = mult_ref.at[pl.ds(rows[0], rows[1] - rows[0])]
        i = number[unit]
        return pltpu.make_async_remote_copy(
            src_ref=src,
            dst_ref=dst,
            send_sem=send_sem.at[colour, i, kind],
            recv_sem=recv_sem.at[colour, i, kind],
            device_id={axis: at(axis, to)},
            device_id_type=MESH,
        )

    def send(colour, unit):
        for kind in (0, 1):
            copy = remote(colour, unit, kind)
            copy.start()
            started.append(copy)

    def arrived(colour, unit):
        for kind in (0, 1):
            remote(colour, unit, kind).wait_recv()
        for kind in (2, 3):
            copy = remote(colour, unit, kind)
            copy.start()
            started.append(copy)

    def arrived_far(colour, unit):
        for kind in (2, 3):
            remote(colour, unit, kind).wait_recv()

    crossings = []

    def cross(colour, second, third):
        axes = ORDERS[colour]
        where = {axes[1]: at(axes[1], second), axes[2]: at(axes[2], third)}
        ref = place(where, rows_of(colour, "all"), me["c"])
        i = ((0, -1, 1, 2).index(second)) * 4 + (0, -1, 1, 2).index(third)
        copy = pltpu.make_async_remote_copy(
            src_ref=ref,
            dst_ref=ref,
            send_sem=sib_send.at[colour, i],
            recv_sem=sib_recv.at[colour, i],
            device_id=other,
            device_id_type=MESH,
        )
        copy.start()
        other_ref = place(where, rows_of(colour, "all"), other["c"])
        arrival = pltpu.make_async_remote_copy(
            src_ref=other_ref,
            dst_ref=other_ref,
            send_sem=sib_send.at[colour, i],
            recv_sem=sib_recv.at[colour, i],
            device_id=other,
            device_id_type=MESH,
        )
        crossings.append((copy, arrival))

    done_leaves = [0]

    def near(count):
        first = done_leaves[0]
        last = min(leaves, first + count)
        done_leaves[0] = last
        if last == first:
            return
        if first == 0:
            own_x.wait()
            for copy in halo:
                copy.wait_recv()

            @pl.when(column == 0)
            def _():
                xbuf[:leaves] = jnp.zeros((leaves,) + xbuf.shape[1:], BF16)

            @pl.when(column == gx - 1)
            def _():
                xbuf[2 * leaves :] = jnp.zeros((leaves,) + xbuf.shape[1:], BF16)

        def body(leaf, carry):
            slot = lax.rem(leaf, depth)
            near_copy(leaf, slot).wait()
            lanes = pl.ds(pl.multiple_of(leaf * panels, panels), panels)
            total = xbuf[leaves + leaf].astype(F32)
            for k in range(slots):
                i = leaf * slots + k
                total = total + live_ref[i] * dot(xbuf[src_ref[i]], nbuf[slot, k], NT)
            base_ref[:, lanes] = total

            @pl.when(leaf + depth < leaves)
            def _():
                near_copy(leaf + depth, slot).start()

            return carry

        lax.fori_loop(first, last, body, 0)

    colours = range(3)
    for unit in (units[0], (1, 0, None), (2, 0, 0)):
        for k in colours:
            send(k, unit)
    keep = pltpu.make_async_copy(
        mult_ref, all_ref.at[me["x"], me["c"], me["y"], me["z"]], own_sem
    )
    keep.start()
    halo = []
    for i, (target, slot) in enumerate(((after, 0), (before, 2))):
        copy = pltpu.make_async_remote_copy(
            src_ref=x_ref,
            dst_ref=xbuf.at[pl.ds(slot * leaves, leaves)],
            send_sem=halo_send.at[i],
            recv_sem=halo_recv.at[i],
            device_id=target,
            device_id_type=MESH,
        )
        copy.start()
        halo.append(copy)

    for k in colours:
        arrived(k, units[0])
        for r in (-1, 1):
            send(k, (1, r, None))
    for k in colours:
        arrived_far(k, units[0])
        send(k, (1, 2, None))
    for k in colours:
        arrived(k, (1, 0, None))
        for r in (-1, 1, 2):
            send(k, (2, r, 0))
    keep.wait()
    for k in colours:
        cross(k, 0, 0)
    for r in (-1, 1, 2):
        for k in colours:
            arrived(k, (1, r, None))
    for k in colours:
        arrived(k, (2, 0, 0))
    for r in (-1, 1):
        for k in colours:
            send(k, (2, None, r))
    for r in (0, -1, 1, 2):
        for k in colours:
            arrived_far(k, (1, r, None))
    for k in colours:
        send(k, (2, None, 2))
    for r in (-1, 1, 2):
        for k in colours:
            cross(k, r, 0)
    near(1)
    for r in (-1, 1, 2):
        for k in colours:
            arrived(k, (2, r, 0))
        near(1)
    for k in colours:
        for t in (-1, 1):
            cross(k, 0, t)
    near(1)
    for r in (-1, 1):
        for k in colours:
            arrived(k, (2, None, r))
            for t in (-1, 1):
                cross(k, r, t)
            near(1)
    for r in (0, -1, 1, 2):
        for k in colours:
            arrived_far(k, (2, r, 0))
        near(1)
    for k in colours:
        cross(k, 0, 2)
    near(leaves)
    for k in colours:
        arrived(k, (2, None, 2))
        for t in (-1, 1):
            cross(k, 2, t)
    for r in (-1, 1, 2):
        for k in colours:
            arrived_far(k, (2, None, r))
            cross(k, r, 2)
    for copy, arrival in crossings:
        arrival.wait_recv()
    for copy, arrival in crossings:
        copy.wait_send()
    for copy in started:
        copy.wait_send()
    for copy in halo:
        copy.wait_send()


def spread(mult, x, near_blocks, near_src, near_count):
    rows, terms = mult.shape
    leaves, slots, panels, _ = near_blocks.shape
    rhs = x.shape[1]
    live = lax.broadcasted_iota(jnp.int32, (leaves, slots), 1) < near_count[:, None]
    tiles = rows // 16
    cuts = (0, 23 * 16, 43 * 16, tiles * 16)
    depth = 4
    hbm = pl.BlockSpec(memory_space=pl.ANY)
    vmem = pl.BlockSpec(memory_space=pltpu.VMEM)
    smem = pl.BlockSpec(memory_space=pltpu.SMEM)
    dma = pltpu.SemaphoreType.DMA
    return pl.pallas_call(
        functools.partial(spread_kernel, cuts),
        in_specs=[vmem, hbm, hbm, smem, smem],
        out_specs=(hbm, vmem),
        out_shape=(
            jax.ShapeDtypeStruct((4, 2, 4, 4, rows, terms), BF16),
            jax.ShapeDtypeStruct((rhs, leaves * panels), F32),
        ),
        scratch_shapes=[
            pltpu.VMEM((3 * leaves, rhs, panels), BF16),
            pltpu.VMEM((depth, slots, panels, panels), BF16),
            dma((3, 12, 4)), dma((3, 12, 4)), dma((3, 16)), dma((3, 16)),
            dma((2,)), dma((2,)), dma, dma, dma((depth,)),
        ],
        compiler_params=pltpu.CompilerParams(
            collective_id=0, has_side_effects=True, vmem_limit_bytes=32 << 20
        ),
        name="spread",
    )(mult, x, near_blocks, near_src.reshape(-1), live.astype(F32).reshape(-1))


def far_kernel(
    src_ref, class_ref, table_ref, all_ref, base_ref, p_ref, m2l_ref, basis_ref,
    image_ref, inner_ref,
    buf, acc, grouped, vbuf, sems, vsem,
):
    leaves, panels, terms = p_ref.shape
    rhs = base_ref.shape[0]
    slots = src_ref.shape[0] // leaves
    classes = m2l_ref.shape[0] // terms
    blocks = basis_ref.shape[0]
    ahead = 4
    group = grouped.shape[0] // rhs

    def entry(i):
        f = src_ref[i]
        sender = f // 4
        leaf = table_ref[sender * 8 + (f - sender * 4)]
        return sender, leaf

    def fetch(leaf):
        def one(e, carry):
            i = leaf * slots + e
            sender, at = entry(i)
            rows = pl.ds(pl.multiple_of(at * rhs, rhs), rhs)
            pltpu.make_async_copy(all_ref.at[sender, rows], buf.at[i], sems.at[leaf]).start()
            return carry

        lax.fori_loop(0, slots, one, 0, unroll=8)

    whole = pltpu.make_async_copy(basis_ref, vbuf, vsem)
    for leaf in range(ahead):
        fetch(leaf)
    whole.start()
    inner_ref[...] = jnp.zeros_like(inner_ref)

    def per_group(g, carry):
        def per_leaf(j, carry):
            leaf = g * group + j

            @pl.when(leaf + ahead < leaves)
            def _():
                fetch(leaf + ahead)

            view = buf.at[pl.ds(leaf * slots, slots)]
            pltpu.make_async_copy(view, view, sems.at[leaf]).wait()
            acc[...] = jnp.zeros_like(acc)

            def one(e, carry):
                i = leaf * slots + e
                f = src_ref[i]
                sender = f // 4
                valid = (f - sender * 4) < table_ref[sender * 8 + 4]
                which = jnp.where(valid, class_ref[i], classes)
                acc[which] += buf[i].astype(F32)
                return carry

            lax.fori_loop(0, slots, one, 0, unroll=8)
            at = pl.ds(pl.multiple_of(j * rhs, rhs), rhs)
            for c in range(classes):
                grouped[at, c * terms : (c + 1) * terms] = acc[c].astype(BF16)
            return carry

        lax.fori_loop(0, group, per_leaf, 0)
        local = dot(grouped[...], m2l_ref[...]).astype(BF16)

        @pl.when(g == 0)
        def _():
            whole.wait()

        for j in range(group):
            leaf = g * group + j
            lanes = pl.ds(pl.multiple_of(leaf * panels, panels), panels)
            far = dot(local[j * rhs : (j + 1) * rhs], p_ref[leaf], NT)
            image = base_ref[:, lanes] + far
            image_ref[:, lanes] = image
            both = jnp.concatenate(halves(image), axis=0)
            v = vbuf[:, :, lanes].reshape(blocks * rhs, panels)
            out = dot(both, v, NT)
            inner_ref[...] += out[:rhs] + out[rhs:]
        return carry

    lax.fori_loop(0, leaves // group, per_group, 0)


def far_field(far_src, far_class, table, everyone, base, p2m, m2l, basis):
    leaves, panels, terms = p2m.shape
    blocks, rhs, columns = basis.shape
    slots = far_src.shape[1]
    classes = m2l.shape[0]
    hbm = pl.BlockSpec(memory_space=pl.ANY)
    vmem = pl.BlockSpec(memory_space=pltpu.VMEM)
    smem = pl.BlockSpec(memory_space=pltpu.SMEM)
    dma = pltpu.SemaphoreType.DMA
    group = 4
    return pl.pallas_call(
        far_kernel,
        in_specs=[smem, smem, smem, hbm, vmem, vmem, vmem, hbm],
        out_specs=(vmem, vmem),
        out_shape=(
            jax.ShapeDtypeStruct((rhs, columns), F32),
            jax.ShapeDtypeStruct((rhs, blocks * rhs), F32),
        ),
        scratch_shapes=[
            pltpu.VMEM((leaves * slots, rhs, terms), BF16),
            pltpu.VMEM((classes + 1, rhs, terms), F32),
            pltpu.VMEM((group * rhs, classes * terms), BF16),
            pltpu.VMEM((blocks, rhs, columns), BF16),
            dma((leaves,)), dma,
        ],
        compiler_params=pltpu.CompilerParams(vmem_limit_bytes=40 << 20),
        name="far_field",
    )(
        far_src.reshape(-1), far_class.reshape(-1), table, everyone, base, p2m,
        m2l.reshape(classes * terms, terms), basis,
    )


def finish_kernel(
    total_rows, inner_ref, image_ref, basis_ref,
    next_ref, proj_ref, factor_ref,
    vbuf, gram_in, one_in, two_in, stack, piece, whole, gone, two_gone,
    s1, r1, s2, r2, s3, r3, vsem,
):
    me = {name: lax.axis_index(name) for name in ALL}
    column = me["x"] * 2 + me["c"]
    segment = me["y"] * 4 + me["z"]
    gx, bulk = 8, 16
    rhs, columns = image_ref.shape
    blocks = basis_ref.shape[0]
    load = pltpu.make_async_copy(basis_ref, vbuf, vsem)
    load.start()

    def col_peer(by):
        c = lax.rem(column + by, gx)
        return c, {"x": c // 2, "c": lax.rem(c, 2)}

    def seg_peer(by):
        s = lax.rem(segment + by, bulk)
        return s, {"y": s // 4, "z": lax.rem(s, 4)}

    barrier = pltpu.get_barrier_semaphore()
    for by in range(1, gx):
        pl.semaphore_signal(barrier, inc=1, device_id=col_peer(by)[1], device_id_type=MESH)
    for by in range(1, bulk):
        pl.semaphore_signal(barrier, inc=1, device_id=seg_peer(by)[1], device_id_type=MESH)
    pl.semaphore_wait(barrier, gx + bulk - 2)

    def remote(src, dst, send, recv, peer):
        return pltpu.make_async_remote_copy(
            src_ref=src, dst_ref=dst, send_sem=send, recv_sem=recv,
            device_id=peer, device_id_type=MESH,
        )

    def all_reduce(n, source, arrivals, mine, parts, result):
        rows = rhs // gx
        sent = []
        for by in range(1, gx):
            c, peer = col_peer(by)
            at = pl.ds(pl.multiple_of(c * rows, rows), rows)
            copy = remote(source.at[at], arrivals.at[gx - by], s1.at[n, by], r1.at[n, gx - by], peer)
            copy.start()
            sent.append(copy)
        own = pl.ds(pl.multiple_of(column * rows, rows), rows)
        total = source[own, :]
        for by in range(1, gx):
            remote(arrivals.at[by], arrivals.at[by], s1.at[n, by], r1.at[n, by], col_peer(1)[1]).wait_recv()
            total = total + arrivals[by]
        mine[...] = total
        for by in range(1, bulk):
            s, peer = seg_peer(by)
            copy = remote(mine, parts.at[segment], s2.at[n, by], r2.at[n, bulk - by], peer)
            copy.start()
            sent.append(copy)
        parts[segment] = total
        for by in range(1, bulk):
            s, peer = seg_peer(by)
            remote(mine, parts.at[s], s2.at[n, by], r2.at[n, by], peer).wait_recv()
        total = parts[0]
        for s in range(1, bulk):
            total = total + parts[s]
        result[own, :] = total
        for by in range(1, gx):
            c, peer = col_peer(by)
            copy = remote(result.at[own], result.at[own], s3.at[n, by], r3.at[n, gx - by], peer)
            copy.start()
            sent.append(copy)
        for by in range(1, gx):
            c, peer = col_peer(by)
            at = pl.ds(pl.multiple_of(c * rows, rows), rows)
            remote(result.at[at], result.at[at], s3.at[n, by], r3.at[n, by], peer).wait_recv()
        for copy in sent:
            copy.wait_send()

    scale = 1.0 / total_rows
    all_reduce(0, inner_ref, one_in, piece, two_in, whole)
    load.wait()
    proj = whole[...] * scale
    coef = jnp.concatenate(halves(proj), axis=0)
    step = 512
    gram = jnp.zeros((2 * rhs, 2 * rhs), F32)
    for i in range(0, columns, step):
        v = vbuf[:, :, i : i + step].reshape(blocks * rhs, step)
        out = dot(coef, v)
        resid = image_ref[:, i : i + step] - (out[:rhs] + out[rhs:])
        both = jnp.concatenate(halves(resid), axis=0)
        stack[:, i : i + step] = both
        gram = gram + dot(both, both, NT)
    gram_in[...] = gram[:rhs] + gram[rhs:]
    for i in range(0, blocks * rhs, 2 * rhs):
        proj_ref[i : i + 2 * rhs, :] = proj[:, i : i + 2 * rhs].T
    all_reduce(1, gram_in, gone, piece.at[:, : 2 * rhs], two_gone, factor_ref)
    folded = factor_ref[...] * scale
    folded = folded + pltpu.roll(folded, rhs, 1)
    lane = lax.broadcasted_iota(jnp.int32, (rhs, 2 * rhs), 1)
    row = lax.broadcasted_iota(jnp.int32, (rhs, 2 * rhs), 0)
    work = jnp.where(lane < rhs, folded, (lane - rhs == row).astype(F32))
    tall = 8
    count = rhs // tall
    part = [work[i * tall : (i + 1) * tall] for i in range(count)]
    low = lax.broadcasted_iota(jnp.int32, (tall, 2 * rhs), 0)
    for b in range(count):
        cols = [
            {i: jnp.broadcast_to(part[i][:, b * tall + t : b * tall + t + 1], (tall, 2 * rhs)) for i in range(b, count)}
            for t in range(tall)
        ]
        for t in range(tall):
            inverse = 1.0 / cols[t][b][t : t + 1, :]
            across = {u: cols[u][b][t : t + 1, :] * inverse for u in range(t + 1, tall)}
            pivot = part[b][t : t + 1, :] * inverse
            for i in range(b, count):
                factor = cols[t][i]
                if i == b:
                    factor = jnp.where(low > t, factor, 0.0)
                part[i] = part[i] - factor * pivot
                for u in range(t + 1, tall):
                    cols[u][i] = cols[u][i] - factor * across[u]
    work = jnp.concatenate(part, axis=0)
    diagonal = jnp.sum(jnp.where(lane == row, work, 0.0), axis=1, keepdims=True)
    work = work * lax.rsqrt(diagonal)
    factor_ref[...] = jnp.where((lane >= row) & (lane < rhs), work, 0.0)
    right = jnp.where(lane < rhs, 0.0, work)
    right = right + pltpu.roll(right, rhs, 1)
    left = jnp.concatenate(halves(right), axis=0)
    for i in range(0, columns, step):
        out = dot(left, stack[:, i : i + step])
        next_ref[:, i : i + step] = (out[:rhs] + out[rhs:]).astype(BF16)


def finish(inner, image, basis, total_rows):
    blocks, rhs, columns = basis.shape
    wide = blocks * rhs
    hbm = pl.BlockSpec(memory_space=pl.ANY)
    vmem = pl.BlockSpec(memory_space=pltpu.VMEM)
    dma = pltpu.SemaphoreType.DMA
    return pl.pallas_call(
        functools.partial(finish_kernel, total_rows),
        in_specs=[vmem, vmem, hbm],
        out_specs=(vmem, vmem, vmem),
        out_shape=(
            jax.ShapeDtypeStruct((rhs, columns), BF16),
            jax.ShapeDtypeStruct((wide, rhs), F32),
            jax.ShapeDtypeStruct((rhs, 2 * rhs), F32),
        ),
        scratch_shapes=[
            pltpu.VMEM((blocks, rhs, columns), BF16),
            pltpu.VMEM((rhs, 2 * rhs), F32),
            pltpu.VMEM((8, 8, wide), F32),
            pltpu.VMEM((16, 8, wide), F32),
            pltpu.VMEM((2 * rhs, columns), BF16),
            pltpu.VMEM((8, wide), F32),
            pltpu.VMEM((rhs, wide), F32),
            pltpu.VMEM((8, 8, 2 * rhs), F32),
            pltpu.VMEM((16, 8, 2 * rhs), F32),
            dma((2, 8)), dma((2, 8)), dma((2, 16)), dma((2, 16)), dma((2, 8)), dma((2, 8)), dma,
        ],
        compiler_params=pltpu.CompilerParams(
            collective_id=1, has_side_effects=True, vmem_limit_bytes=32 << 20
        ),
        name="finish",
    )(inner, image, basis)


def shards(
    basis, near_blocks, near_src, near_count, p2m, m2l, send_list, send_count, far_src, far_class
):
    blocks, rhs, columns = basis.shape
    leaves, panels, terms = p2m.shape
    peers = lax.axis_size(ALL)
    slots = send_list.shape[2]
    mult, x = multipoles(basis, p2m, send_list, send_count)
    everyone, base = spread(mult, x, near_blocks, near_src, near_count)
    everyone = everyone.reshape(peers, *mult.shape)
    rows = leaves * rhs
    lists = lax.slice(everyone, (0, rows, 0), (peers, rows + 8, terms))
    me = lax.axis_index(ALL)
    table = lax.dynamic_slice_in_dim(lists, me, 1, axis=2).astype(jnp.int32).reshape(-1)
    image, inner = far_field(far_src, far_class, table, everyone, base, p2m, m2l, basis)
    new, proj, upper = finish(inner, image, basis, columns * peers)
    factor = upper[:, :rhs].T
    return (new, proj.reshape(blocks, rhs, rhs), factor)


def solution(mesh):
    finer = Mesh(mesh.devices.reshape(4, 2, 4, 4), ALL)
    in_specs = (
        P(None, None, ALL),
        P(ALL, None, None, None),
        P(ALL, None),
        P(ALL),
        P(ALL, None, None),
        P(),
        P(ALL, None, None),
        P(ALL, None),
        P(ALL, None),
        P(ALL, None),
    )
    out_specs = (P(None, ALL), P(), P())
    return jax.shard_map(
        shards, mesh=finer, in_specs=in_specs, out_specs=out_specs, check_vma=False
    )
```

```python
import functools

import jax
import jax.numpy as jnp
from jax import lax
from jax.experimental import pallas as pl
from jax.experimental.pallas import tpu as pltpu
from jax.sharding import Mesh
from jax.sharding import PartitionSpec as P

ALL = ("x", "c", "y", "z")
ORDERS = (("x", "y", "z"), ("y", "z", "x"), ("z", "x", "y"))
MESH = pl.DeviceIdType.MESH
F32, BF16 = jnp.float32, jnp.bfloat16
LIMIT = 67043328
NT = (((1,), (1,)), ((), ()))
TN = (((0,), (0,)), ((), ()))


def dot(a, b, dims=(((1,), (0,)), ((), ()))):
    return lax.dot_general(a, b, dims, preferred_element_type=F32)


def halves(values):
    upper = values.astype(BF16)
    return upper, (values - upper.astype(F32)).astype(BF16)


def spread_kernel(
    cuts, basis_ref, p_ref, near_blocks_ref, list_ref, count_ref, src_ref, near_count_ref,
    all_ref, base_ref, table_ref,
    xbuf, nbuf, pbuf, mbuf, stage, lists,
    send_sem, recv_sem, sib_send, sib_recv, halo_send, halo_recv, list_send, list_recv,
    own_sem, x_sem, p_sem, stage_sem, nsem,
):
    me = {name: lax.axis_index(name) for name in ALL}
    leaves = near_blocks_ref.shape[0]
    slots = near_blocks_ref.shape[1]
    panels = near_blocks_ref.shape[2]
    depth = nbuf.shape[0]
    column = me["x"] * 2 + me["c"]

    def at(axis, by):
        return lax.rem(me[axis] + (by + 4), 4)

    def near_copy(leaf, slot):
        return pltpu.make_async_copy(near_blocks_ref.at[leaf], nbuf.at[slot], nsem.at[slot])

    blocks, rhs = basis_ref.shape[:2]
    mine = xbuf.at[pl.ds(leaves, leaves)]
    for leaf in range(leaves):
        pltpu.make_async_copy(
            basis_ref.at[blocks - 1, :, pl.ds(leaf * panels, panels)], mine.at[leaf], x_sem
        ).start()
    load_p = pltpu.make_async_copy(p_ref, pbuf, p_sem)
    load_p.start()
    for leaf in range(depth):
        near_copy(leaf, leaf).start()

    other = {"c": 1 - me["c"]}
    barrier = pltpu.get_barrier_semaphore()
    peers = [{axis: at(axis, by)} for axis in ("x", "y", "z") for by in (1, -1)]
    peers.append(other)
    gx = 8
    after_col = lax.rem(column + 1, gx)
    before_col = lax.rem(column + gx - 1, gx)
    after = {"x": after_col // 2, "c": lax.rem(after_col, 2)}
    before = {"x": before_col // 2, "c": lax.rem(before_col, 2)}
    peers += [after, before] + [{axis: at(axis, 2)} for axis in ("x", "y", "z")]
    for peer in peers:
        pl.semaphore_signal(barrier, inc=1, device_id=peer, device_id_type=MESH)
    slots_out = list_ref.shape[1]
    stage[...] = jnp.zeros_like(stage)
    stage[:slots_out, :] = list_ref[0]
    stage[slots_out : slots_out + 1, :] = count_ref[...]
    pltpu.make_async_copy(mine, mine, x_sem).wait()
    load_p.wait()

    def multipole(leaf, carry):
        rows = pl.ds(pl.multiple_of(leaf * rhs, rhs), rhs)
        mbuf[rows, :] = dot(xbuf[leaves + leaf], pbuf[leaf]).astype(BF16)
        return carry

    lax.fori_loop(0, leaves, multipole, 0, unroll=4)
    here = all_ref.at[me["x"], me["c"], me["y"], me["z"]]
    keep = pltpu.make_async_copy(mbuf, here, own_sem)
    keep.start()
    my_list = lists.at[me["x"], me["c"], me["y"], me["z"]]
    keep_list = pltpu.make_async_copy(stage, my_list, stage_sem)
    keep_list.start()
    pl.semaphore_wait(barrier, len(peers))

    def place(where, rows, core):
        index = []
        for name in ALL:
            if name == "c":
                index.append(core)
            elif name in where:
                index.append(where[name])
            else:
                index.append(slice(None))
        return all_ref.at[tuple(index) + (pl.ds(rows[0], rows[1] - rows[0]),)]

    units = [(0, None, None)]
    units += [(1, r, None) for r in (0, -1, 1, 2)]
    units += [(2, r, 0) for r in (0, -1, 1, 2)]
    units += [(2, None, r) for r in (-1, 1, 2)]
    number = {u: i for i, u in enumerate(units)}
    started = []

    def where_of(colour, unit, by):
        axes = ORDERS[colour]
        phase, first, second = unit
        where = {}
        if phase == 0:
            where = {axes[0]: by, axes[1]: 0, axes[2]: 0}
        elif phase == 1:
            where = {axes[0]: first, axes[1]: by, axes[2]: 0}
        else:
            where = {axes[1]: second, axes[2]: by}
            if first is not None:
                where[axes[0]] = first
        return where

    def rows_of(colour, part):
        low, high = cuts[colour], cuts[colour + 1]
        middle = low + (high - low) // 32 * 16
        return {"all": (low, high), "lower": (low, middle), "upper": (middle, high)}[part]

    def remote(colour, unit, kind):
        axis = ORDERS[colour][unit[0]]
        by, to, part = ((0, 1, "all"), (0, -1, "all"), (-1, 1, "lower"), (1, -1, "upper"))[kind]
        offsets = where_of(colour, unit, by)
        where = {name: at(name, v) for name, v in offsets.items()}
        rows = rows_of(colour, part)
        dst = place(where, rows, me["c"])
        i = number[unit]
        return pltpu.make_async_remote_copy(
            src_ref=dst,
            dst_ref=dst,
            send_sem=send_sem.at[colour, i, kind],
            recv_sem=recv_sem.at[colour, i, kind],
            device_id={axis: at(axis, to)},
            device_id_type=MESH,
        )

    def send(colour, unit):
        for kind in (0, 1):
            copy = remote(colour, unit, kind)
            copy.start()
            started.append(copy)

    def arrived(colour, unit):
        for kind in (0, 1):
            remote(colour, unit, kind).wait_recv()
        for kind in (2, 3):
            copy = remote(colour, unit, kind)
            copy.start()
            started.append(copy)

    def arrived_far(colour, unit):
        for kind in (2, 3):
            remote(colour, unit, kind).wait_recv()

    crossings = []

    def cross(colour, second, third):
        axes = ORDERS[colour]
        where = {axes[1]: at(axes[1], second), axes[2]: at(axes[2], third)}
        ref = place(where, rows_of(colour, "all"), me["c"])
        i = ((0, -1, 1, 2).index(second)) * 4 + (0, -1, 1, 2).index(third)
        copy = pltpu.make_async_remote_copy(
            src_ref=ref,
            dst_ref=ref,
            send_sem=sib_send.at[colour, i],
            recv_sem=sib_recv.at[colour, i],
            device_id=other,
            device_id_type=MESH,
        )
        copy.start()
        other_ref = place(where, rows_of(colour, "all"), other["c"])
        arrival = pltpu.make_async_remote_copy(
            src_ref=other_ref,
            dst_ref=other_ref,
            send_sem=sib_send.at[colour, i],
            recv_sem=sib_recv.at[colour, i],
            device_id=other,
            device_id_type=MESH,
        )
        crossings.append((copy, arrival))

    done_leaves = [0]

    def near(count):
        first = done_leaves[0]
        last = min(leaves, first + count)
        done_leaves[0] = last
        if last == first:
            return
        if first == 0:
            for copy in halo:
                copy.wait_recv()

            @pl.when(column == 0)
            def _():
                xbuf[:leaves] = jnp.zeros((leaves,) + xbuf.shape[1:], BF16)

            @pl.when(column == gx - 1)
            def _():
                xbuf[2 * leaves :] = jnp.zeros((leaves,) + xbuf.shape[1:], BF16)

        def body(leaf, carry):
            slot = lax.rem(leaf, depth)
            near_copy(leaf, slot).wait()
            lanes = pl.ds(pl.multiple_of(leaf * panels, panels), panels)
            total = xbuf[leaves + leaf].astype(F32)
            for k in range(slots):
                live = lax.min(lax.max(near_count_ref[leaf] - k, 0), 1).astype(F32)
                total = total + live * dot(xbuf[src_ref[k, leaf]], nbuf[slot, k], NT)
            base_ref[:, lanes] = total

            @pl.when(leaf + depth < leaves)
            def _():
                near_copy(leaf + depth, slot).start()

            return carry

        lax.fori_loop(first, last, body, 0)

    def list_region(stage_index):
        index = [me["x"], me["c"], me["y"], me["z"]]
        for place_of in ((), (0,), (0, 2), (0, 2, 3))[stage_index]:
            index[place_of] = slice(None)
        return lists.at[tuple(index)]

    def list_copies(i):
        if i == 3:
            targets = [other]
        else:
            axis = ("x", "y", "z")[i]
            targets = [{axis: at(axis, by)} for by in (1, 2, 3)]
        region = list_region(i)
        out = []
        for t, target in enumerate(targets):
            out.append(
                pltpu.make_async_remote_copy(
                    src_ref=region, dst_ref=region,
                    send_sem=list_send.at[i, t], recv_sem=list_recv.at[i, t],
                    device_id=target, device_id_type=MESH,
                )
            )
        return out

    list_sent = []

    def lists_go(i):
        for copy in list_copies(i):
            copy.start()
            list_sent.append(copy)

    def lists_come(i):
        for copy in list_copies(i):
            copy.wait_recv()

    colours = range(3)
    keep.wait()
    keep_list.wait()
    lists_go(0)
    for unit in (units[0], (1, 0, None), (2, 0, 0)):
        for k in colours:
            send(k, unit)
    halo = []
    for i, (target, slot) in enumerate(((after, 0), (before, 2))):
        copy = pltpu.make_async_remote_copy(
            src_ref=mine,
            dst_ref=xbuf.at[pl.ds(slot * leaves, leaves)],
            send_sem=halo_send.at[i],
            recv_sem=halo_recv.at[i],
            device_id=target,
            device_id_type=MESH,
        )
        copy.start()
        halo.append(copy)

    for k in colours:
        arrived(k, units[0])
        for r in (-1, 1):
            send(k, (1, r, None))
    for k in colours:
        arrived_far(k, units[0])
        send(k, (1, 2, None))
    for k in colours:
        arrived(k, (1, 0, None))
        for r in (-1, 1, 2):
            send(k, (2, r, 0))
    for k in colours:
        cross(k, 0, 0)
    lists_come(0)
    lists_go(1)
    for r in (-1, 1, 2):
        for k in colours:
            arrived(k, (1, r, None))
    for k in colours:
        arrived(k, (2, 0, 0))
    for r in (-1, 1):
        for k in colours:
            send(k, (2, None, r))
    for r in (0, -1, 1, 2):
        for k in colours:
            arrived_far(k, (1, r, None))
    for k in colours:
        send(k, (2, None, 2))
    for r in (-1, 1, 2):
        for k in colours:
            cross(k, r, 0)
    lists_come(1)
    lists_go(2)
    near(1)
    for r in (-1, 1, 2):
        for k in colours:
            arrived(k, (2, r, 0))
        near(1)
    lists_come(2)
    lists_go(3)
    for k in colours:
        for t in (-1, 1):
            cross(k, 0, t)
    near(1)
    for r in (-1, 1):
        for k in colours:
            arrived(k, (2, None, r))
            for t in (-1, 1):
                cross(k, r, t)
            near(1)
    for r in (0, -1, 1, 2):
        for k in colours:
            arrived_far(k, (2, r, 0))
        near(1)
    for k in colours:
        cross(k, 0, 2)
    near(leaves)
    lists_come(3)
    index = ((me["x"] * 2 + me["c"]) * 4 + me["y"]) * 4 + me["z"]
    peers_all = lists.shape[-1]
    mark = (lax.broadcasted_iota(jnp.int32, (8, peers_all), 1) == index).astype(BF16)
    table = dot(mark, lists[...].reshape(-1, peers_all).astype(F32).astype(BF16), NT)
    table_ref[...] = table[:1].astype(jnp.int32)
    for k in colours:
        arrived(k, (2, None, 2))
        for t in (-1, 1):
            cross(k, 2, t)
    for r in (-1, 1, 2):
        for k in colours:
            arrived_far(k, (2, None, r))
            cross(k, r, 2)
    for copy, arrival in crossings:
        arrival.wait_recv()
    for copy, arrival in crossings:
        copy.wait_send()
    for copy in started + list_sent:
        copy.wait_send()
    for copy in halo:
        copy.wait_send()


def spread(basis, p2m, near_blocks, send_list, send_count, near_src, near_count):
    leaves, slots, panels, _ = near_blocks.shape
    rhs = basis.shape[1]
    terms = p2m.shape[2]
    rows = leaves * rhs
    peers = send_list.shape[1]
    tiles = rows // 16
    cuts = (0, 22 * 16, 42 * 16, tiles * 16)
    depth = 4
    hbm = pl.BlockSpec(memory_space=pltpu.HBM)
    vmem = pl.BlockSpec(memory_space=pltpu.VMEM)
    smem = pl.BlockSpec(memory_space=pltpu.SMEM)
    dma = pltpu.SemaphoreType.DMA
    return pl.pallas_call(
        functools.partial(spread_kernel, cuts),
        in_specs=[hbm, hbm, hbm, vmem, vmem, smem, smem],
        out_specs=(hbm, vmem, vmem),
        out_shape=(
            jax.ShapeDtypeStruct((4, 2, 4, 4, rows, terms), BF16),
            jax.ShapeDtypeStruct((rhs, leaves * panels), F32),
            jax.ShapeDtypeStruct((1, peers * 8), jnp.int32),
        ),
        scratch_shapes=[
            pltpu.VMEM((3 * leaves, rhs, panels), BF16),
            pltpu.VMEM((depth, slots, panels, panels), BF16),
            pltpu.VMEM((leaves, panels, terms), BF16),
            pltpu.VMEM((rows, terms), BF16),
            pltpu.VMEM((8, peers), jnp.int32),
            pltpu.VMEM((4, 2, 4, 4, 8, peers), jnp.int32),
            dma((3, 12, 4)), dma((3, 12, 4)), dma((3, 16)), dma((3, 16)),
            dma((2,)), dma((2,)), dma((4, 3)), dma((4, 3)),
            dma, dma, dma, dma, dma((depth,)),
        ],
        compiler_params=pltpu.CompilerParams(
            collective_id=0, has_side_effects=True, vmem_limit_bytes=20 << 20
        ),
        name="spread",
    )(
        basis, p2m, near_blocks, jnp.swapaxes(send_list, 1, 2), send_count,
        near_src.T, near_count,
    )


def far_kernel(
    src_ref, class_ref, table_ref, all_ref, base_ref, p_hbm, m2l_hbm, basis_ref,
    image_ref, inner_ref,
    buf, acc_a, acc_b, grouped, vbuf, p_ref, m2l_ref, sems, vsem,
):
    leaves, panels, terms = p_ref.shape
    rhs = base_ref.shape[0]
    slots = src_ref.shape[1]
    classes = m2l_ref.shape[0] // terms
    blocks = basis_ref.shape[0]
    ahead = 4
    group = grouped.shape[0] // rhs

    def fetch(leaf):
        def one(e, carry):
            f = src_ref[leaf, e]
            sender = lax.shift_right_logical(f, 2)
            at = table_ref[0, sender * 8 + (f & 3)]
            rows = pl.ds(pl.multiple_of(at * rhs, rhs), rhs)
            pltpu.make_async_copy(
                all_ref.at[sender, rows], buf.at[leaf * slots + e], sems.at[leaf]
            ).start()
            return carry

        lax.fori_loop(0, slots, one, 0, unroll=8)

    loads = [
        pltpu.make_async_copy(a, b, vsem.at[i])
        for i, (a, b) in enumerate(((m2l_hbm, m2l_ref), (p_hbm, p_ref), (basis_ref, vbuf)))
    ]
    for leaf in range(ahead):
        fetch(leaf)
    for load in loads:
        load.start()
    inner_ref[...] = jnp.zeros_like(inner_ref)

    def per_group(g, carry):
        def per_pair(j, carry):
            first = g * group + j * 2

            @pl.when(first + ahead < leaves)
            def _():
                fetch(first + ahead)
                fetch(first + ahead + 1)

            for by in range(2):
                view = buf.at[pl.ds((first + by) * slots, slots)]
                pltpu.make_async_copy(view, view, sems.at[first + by]).wait()
            acc_a[...] = jnp.zeros_like(acc_a)
            acc_b[...] = jnp.zeros_like(acc_b)

            def one(e, carry):
                for acc, leaf in ((acc_a, first), (acc_b, first + 1)):
                    f = src_ref[leaf, e]
                    sender = lax.shift_right_logical(f, 2)
                    valid = (f & 3) < table_ref[0, sender * 8 + 4]
                    which = jnp.where(valid, class_ref[leaf, e], classes)
                    acc[which] += buf[leaf * slots + e].astype(F32)
                return carry

            lax.fori_loop(0, slots, one, 0, unroll=4)
            for by, acc in ((0, acc_a), (1, acc_b)):
                at = pl.ds(pl.multiple_of((j * 2 + by) * rhs, rhs), rhs)
                for c in range(classes):
                    grouped[at, c * terms : (c + 1) * terms] = acc[c].astype(BF16)
            return carry

        lax.fori_loop(0, group // 2, per_pair, 0)

        @pl.when(g == 0)
        def _():
            for load in loads:
                load.wait()

        local = dot(grouped[...], m2l_ref[...]).astype(BF16)

        for j in range(group):
            leaf = g * group + j
            lanes = pl.ds(pl.multiple_of(leaf * panels, panels), panels)
            far = dot(local[j * rhs : (j + 1) * rhs], p_ref[leaf], NT)
            image = base_ref[:, lanes] + far
            image_ref[:, lanes] = image
            both = jnp.concatenate(halves(image), axis=0)
            v = vbuf[:, :, lanes].reshape(blocks * rhs, panels)
            out = dot(both, v, NT)
            inner_ref[...] += out[:rhs] + out[rhs:]
        return carry

    lax.fori_loop(0, leaves // group, per_group, 0)


def far_field(far_src, far_class, table, everyone, base, p2m, m2l, basis):
    leaves, panels, terms = p2m.shape
    blocks, rhs, columns = basis.shape
    slots = far_src.shape[1]
    classes = m2l.shape[0]
    hbm = pl.BlockSpec(memory_space=pltpu.HBM)
    vmem = pl.BlockSpec(memory_space=pltpu.VMEM)
    smem = pl.BlockSpec(memory_space=pltpu.SMEM)
    dma = pltpu.SemaphoreType.DMA
    group = 4
    return pl.pallas_call(
        far_kernel,
        in_specs=[smem, smem, smem, hbm, vmem, hbm, hbm, hbm],
        out_specs=(vmem, vmem),
        out_shape=(
            jax.ShapeDtypeStruct((rhs, columns), F32),
            jax.ShapeDtypeStruct((rhs, blocks * rhs), F32),
        ),
        scratch_shapes=[
            pltpu.VMEM((leaves * slots, rhs, terms), BF16),
            pltpu.VMEM((classes + 1, rhs, terms), F32),
            pltpu.VMEM((classes + 1, rhs, terms), F32),
            pltpu.VMEM((group * rhs, classes * terms), BF16),
            pltpu.VMEM((blocks, rhs, columns), BF16),
            pltpu.VMEM((leaves, panels, terms), BF16),
            pltpu.VMEM((classes * terms, terms), BF16),
            dma((leaves,)), dma((3,)),
        ],
        compiler_params=pltpu.CompilerParams(vmem_limit_bytes=28 << 20),
        name="far_field",
    )(
        far_src, far_class, table, everyone, base, p2m,
        m2l.reshape(classes * terms, terms), basis,
    )


def finish_kernel(
    total_rows, inner_ref, image_ref, basis_ref,
    next_ref, proj_ref, factor_ref,
    vbuf, gram_in, one_in, two_in, stack, piece, whole, gone, two_gone,
    s1, r1, s2, r2, s3, r3, vsem,
):
    me = {name: lax.axis_index(name) for name in ALL}
    column = me["x"] * 2 + me["c"]
    segment = me["y"] * 4 + me["z"]
    gx, bulk = 8, 16
    rhs, columns = image_ref.shape
    blocks = basis_ref.shape[0]
    load = pltpu.make_async_copy(basis_ref, vbuf, vsem)
    load.start()

    def col_peer(by):
        c = lax.rem(column + by, gx)
        return c, {"x": c // 2, "c": lax.rem(c, 2)}

    def seg_peer(by):
        s = lax.rem(segment + by, bulk)
        return s, {"y": s // 4, "z": lax.rem(s, 4)}

    barrier = pltpu.get_barrier_semaphore()
    for by in range(1, gx):
        pl.semaphore_signal(barrier, inc=1, device_id=col_peer(by)[1], device_id_type=MESH)
    for by in range(1, bulk):
        pl.semaphore_signal(barrier, inc=1, device_id=seg_peer(by)[1], device_id_type=MESH)
    pl.semaphore_wait(barrier, gx + bulk - 2)

    def remote(src, dst, send, recv, peer):
        return pltpu.make_async_remote_copy(
            src_ref=src, dst_ref=dst, send_sem=send, recv_sem=recv,
            device_id=peer, device_id_type=MESH,
        )

    def all_reduce(n, source, arrivals, mine, parts, result):
        rows = rhs // gx
        sent = []
        for by in range(1, gx):
            c, peer = col_peer(by)
            at = pl.ds(pl.multiple_of(c * rows, rows), rows)
            copy = remote(source.at[at], arrivals.at[gx - by], s1.at[n, by], r1.at[n, gx - by], peer)
            copy.start()
            sent.append(copy)
        own = pl.ds(pl.multiple_of(column * rows, rows), rows)
        total = source[own, :]
        for by in range(1, gx):
            remote(arrivals.at[by], arrivals.at[by], s1.at[n, by], r1.at[n, by], col_peer(1)[1]).wait_recv()
            total = total + arrivals[by]
        mine[...] = total
        for by in range(1, bulk):
            s, peer = seg_peer(by)
            copy = remote(mine, parts.at[segment], s2.at[n, by], r2.at[n, bulk - by], peer)
            copy.start()
            sent.append(copy)
        parts[segment] = total
        for by in range(1, bulk):
            s, peer = seg_peer(by)
            remote(mine, parts.at[s], s2.at[n, by], r2.at[n, by], peer).wait_recv()
        total = parts[0]
        for s in range(1, bulk):
            total = total + parts[s]
        result[own, :] = total
        for by in range(1, gx):
            c, peer = col_peer(by)
            copy = remote(result.at[own], result.at[own], s3.at[n, by], r3.at[n, gx - by], peer)
            copy.start()
            sent.append(copy)
        for by in range(1, gx):
            c, peer = col_peer(by)
            at = pl.ds(pl.multiple_of(c * rows, rows), rows)
            remote(result.at[at], result.at[at], s3.at[n, by], r3.at[n, by], peer).wait_recv()
        for copy in sent:
            copy.wait_send()

    scale = 1.0 / total_rows
    all_reduce(0, inner_ref, one_in, piece, two_in, whole)
    load.wait()
    proj = whole[...] * scale
    coef = jnp.concatenate(halves(proj), axis=0)
    step = 512
    gram = jnp.zeros((2 * rhs, 2 * rhs), F32)
    for i in range(0, columns, step):
        v = vbuf[:, :, i : i + step].reshape(blocks * rhs, step)
        out = dot(coef, v)
        resid = image_ref[:, i : i + step] - (out[:rhs] + out[rhs:])
        both = jnp.concatenate(halves(resid), axis=0)
        stack[:, i : i + step] = both
        gram = gram + dot(both, both, NT)
    gram_in[...] = gram[:rhs] + gram[rhs:]
    for i in range(0, blocks * rhs, 2 * rhs):
        proj_ref[i : i + 2 * rhs, :] = proj[:, i : i + 2 * rhs].T
    all_reduce(1, gram_in, gone, piece.at[:, : 2 * rhs], two_gone, factor_ref)
    folded = factor_ref[...] * scale
    folded = folded + pltpu.roll(folded, rhs, 1)
    lane = lax.broadcasted_iota(jnp.int32, (rhs, 2 * rhs), 1)
    row = lax.broadcasted_iota(jnp.int32, (rhs, 2 * rhs), 0)
    work = jnp.where(lane < rhs, folded, (lane - rhs == row).astype(F32))
    tall = 8
    count = rhs // tall
    part = [work[i * tall : (i + 1) * tall] for i in range(count)]
    low = lax.broadcasted_iota(jnp.int32, (tall, 2 * rhs), 0)
    for b in range(count):
        cols = [
            {i: jnp.broadcast_to(part[i][:, b * tall + t : b * tall + t + 1], (tall, 2 * rhs)) for i in range(b, count)}
            for t in range(tall)
        ]
        for t in range(tall):
            inverse = 1.0 / cols[t][b][t : t + 1, :]
            across = {u: cols[u][b][t : t + 1, :] * inverse for u in range(t + 1, tall)}
            pivot = part[b][t : t + 1, :] * inverse
            for i in range(b, count):
                factor = cols[t][i]
                if i == b:
                    factor = jnp.where(low > t, factor, 0.0)
                part[i] = part[i] - factor * pivot
                for u in range(t + 1, tall):
                    cols[u][i] = cols[u][i] - factor * across[u]
    work = jnp.concatenate(part, axis=0)
    diagonal = jnp.sum(jnp.where(lane == row, work, 0.0), axis=1, keepdims=True)
    work = work * lax.rsqrt(diagonal)
    factor_ref[...] = jnp.where((lane >= row) & (lane < rhs), work, 0.0)
    right = jnp.where(lane < rhs, 0.0, work)
    right = right + pltpu.roll(right, rhs, 1)
    left = jnp.concatenate(halves(right), axis=0)
    for i in range(0, columns, step):
        out = dot(left, stack[:, i : i + step])
        next_ref[:, i : i + step] = (out[:rhs] + out[rhs:]).astype(BF16)


def finish(inner, image, basis, total_rows):
    blocks, rhs, columns = basis.shape
    wide = blocks * rhs
    hbm = pl.BlockSpec(memory_space=pltpu.HBM)
    vmem = pl.BlockSpec(memory_space=pltpu.VMEM)
    dma = pltpu.SemaphoreType.DMA
    return pl.pallas_call(
        functools.partial(finish_kernel, total_rows),
        in_specs=[vmem, vmem, hbm],
        out_specs=(vmem, vmem, vmem),
        out_shape=(
            jax.ShapeDtypeStruct((rhs, columns), BF16),
            jax.ShapeDtypeStruct((wide, rhs), F32),
            jax.ShapeDtypeStruct((rhs, 2 * rhs), F32),
        ),
        scratch_shapes=[
            pltpu.VMEM((blocks, rhs, columns), BF16),
            pltpu.VMEM((rhs, 2 * rhs), F32),
            pltpu.VMEM((8, 8, wide), F32),
            pltpu.VMEM((16, 8, wide), F32),
            pltpu.VMEM((2 * rhs, columns), BF16),
            pltpu.VMEM((8, wide), F32),
            pltpu.VMEM((rhs, wide), F32),
            pltpu.VMEM((8, 8, 2 * rhs), F32),
            pltpu.VMEM((16, 8, 2 * rhs), F32),
            dma((2, 8)), dma((2, 8)), dma((2, 16)), dma((2, 16)), dma((2, 8)), dma((2, 8)), dma,
        ],
        compiler_params=pltpu.CompilerParams(
            collective_id=1, has_side_effects=True, vmem_limit_bytes=20 << 20
        ),
        name="finish",
    )(inner, image, basis)


def shards(
    basis, near_blocks, near_src, near_count, p2m, m2l, send_list, send_count, far_src, far_class
):
    blocks, rhs, columns = basis.shape
    leaves, panels, terms = p2m.shape
    peers = lax.axis_size(ALL)
    everyone, base, table = spread(
        basis, p2m, near_blocks, send_list, send_count, near_src, near_count
    )
    everyone = everyone.reshape(peers, leaves * rhs, terms)
    image, inner = far_field(far_src, far_class, table, everyone, base, p2m, m2l, basis)
    new, proj, upper = finish(inner, image, basis, columns * peers)
    factor = upper[:, :rhs].T
    return (new, proj.reshape(blocks, rhs, rhs), factor)


def solution(mesh):
    finer = Mesh(mesh.devices.reshape(4, 2, 4, 4), ALL)
    in_specs = (
        P(None, None, ALL),
        P(ALL, None, None, None),
        P(ALL, None),
        P(ALL),
        P(ALL, None, None),
        P(),
        P(ALL, None, None),
        P(ALL, None),
        P(ALL, None),
        P(ALL, None),
    )
    out_specs = (P(None, ALL), P(), P())
    return jax.shard_map(
        shards, mesh=finer, in_specs=in_specs, out_specs=out_specs, check_vma=False
    )
```

```python
import functools

import jax
import jax.numpy as jnp
from jax import lax
from jax.experimental import pallas as pl
from jax.experimental.pallas import tpu as pltpu
from jax.sharding import Mesh
from jax.sharding import PartitionSpec as P

ALL = ("x", "c", "y", "z")
ORDERS = (("x", "y", "z"), ("y", "z", "x"), ("z", "x", "y"))
MESH = pl.DeviceIdType.MESH
F32, BF16 = jnp.float32, jnp.bfloat16
LIMIT = 67043328
NT = (((1,), (1,)), ((), ()))
TN = (((0,), (0,)), ((), ()))


def dot(a, b, dims=(((1,), (0,)), ((), ()))):
    return lax.dot_general(a, b, dims, preferred_element_type=F32)


def halves(values):
    upper = values.astype(BF16)
    return upper, (values - upper.astype(F32)).astype(BF16)


def spread_kernel(
    cuts, basis_ref, p_ref, near_blocks_ref, list_ref, count_ref, src_ref, near_count_ref,
    all_ref, base_ref, table_ref,
    xbuf, nbuf, pbuf, mbuf, stage, lists,
    send_sem, recv_sem, sib_send, sib_recv, halo_send, halo_recv, list_send, list_recv,
    own_sem, x_sem, p_sem, stage_sem, nsem,
):
    me = {name: lax.axis_index(name) for name in ALL}
    leaves = near_blocks_ref.shape[0]
    slots = near_blocks_ref.shape[1]
    panels = near_blocks_ref.shape[2]
    depth = nbuf.shape[0]
    column = me["x"] * 2 + me["c"]

    def at(axis, by):
        return lax.rem(me[axis] + (by + 4), 4)

    def near_copy(leaf, slot):
        return pltpu.make_async_copy(near_blocks_ref.at[leaf], nbuf.at[slot], nsem.at[slot])

    blocks, rhs = basis_ref.shape[:2]
    mine = xbuf.at[pl.ds(leaves, leaves)]
    for leaf in range(leaves):
        pltpu.make_async_copy(
            basis_ref.at[blocks - 1, :, pl.ds(leaf * panels, panels)], mine.at[leaf], x_sem
        ).start()
    load_p = pltpu.make_async_copy(p_ref, pbuf, p_sem)
    load_p.start()
    for leaf in range(depth):
        near_copy(leaf, leaf).start()

    other = {"c": 1 - me["c"]}
    barrier = pltpu.get_barrier_semaphore()
    peers = [{axis: at(axis, by)} for axis in ("x", "y", "z") for by in (1, -1)]
    peers.append(other)
    gx = 8
    after_col = lax.rem(column + 1, gx)
    before_col = lax.rem(column + gx - 1, gx)
    after = {"x": after_col // 2, "c": lax.rem(after_col, 2)}
    before = {"x": before_col // 2, "c": lax.rem(before_col, 2)}
    peers += [after, before] + [{axis: at(axis, 2)} for axis in ("x", "y", "z")]
    for peer in peers:
        pl.semaphore_signal(barrier, inc=1, device_id=peer, device_id_type=MESH)
    slots_out = list_ref.shape[1]
    stage[...] = jnp.zeros_like(stage)
    stage[:slots_out, :] = list_ref[0]
    stage[slots_out : slots_out + 1, :] = count_ref[...]
    pltpu.make_async_copy(mine, mine, x_sem).wait()
    pl.semaphore_wait(barrier, len(peers))
    halo = []
    for i, (target, slot) in enumerate(((after, 0), (before, 2))):
        copy = pltpu.make_async_remote_copy(
            src_ref=mine,
            dst_ref=xbuf.at[pl.ds(slot * leaves, leaves)],
            send_sem=halo_send.at[i],
            recv_sem=halo_recv.at[i],
            device_id=target,
            device_id_type=MESH,
        )
        copy.start()
        halo.append(copy)
    load_p.wait()

    def multipole(leaf, carry):
        rows = pl.ds(pl.multiple_of(leaf * rhs, rhs), rhs)
        mbuf[rows, :] = dot(xbuf[leaves + leaf], pbuf[leaf]).astype(BF16)
        return carry

    lax.fori_loop(0, leaves, multipole, 0, unroll=4)
    here = all_ref.at[me["x"], me["c"], me["y"], me["z"]]
    keep = pltpu.make_async_copy(mbuf, here, own_sem)
    keep.start()
    my_list = lists.at[me["x"], me["c"], me["y"], me["z"]]
    keep_list = pltpu.make_async_copy(stage, my_list, stage_sem)
    keep_list.start()

    def place(where, rows, core):
        index = []
        for name in ALL:
            if name == "c":
                index.append(core)
            elif name in where:
                index.append(where[name])
            else:
                index.append(slice(None))
        return all_ref.at[tuple(index) + (pl.ds(rows[0], rows[1] - rows[0]),)]

    units = [(0, None, None)]
    units += [(1, r, None) for r in (0, -1, 1, 2)]
    units += [(2, r, 0) for r in (0, -1, 1, 2)]
    units += [(2, None, r) for r in (-1, 1, 2)]
    number = {u: i for i, u in enumerate(units)}
    started = []

    def where_of(colour, unit, by):
        axes = ORDERS[colour]
        phase, first, second = unit
        where = {}
        if phase == 0:
            where = {axes[0]: by, axes[1]: 0, axes[2]: 0}
        elif phase == 1:
            where = {axes[0]: first, axes[1]: by, axes[2]: 0}
        else:
            where = {axes[1]: second, axes[2]: by}
            if first is not None:
                where[axes[0]] = first
        return where

    def rows_of(colour, part):
        low, high = cuts[colour], cuts[colour + 1]
        middle = low + (high - low) // 32 * 16
        return {"all": (low, high), "lower": (low, middle), "upper": (middle, high)}[part]

    def remote(colour, unit, kind):
        axis = ORDERS[colour][unit[0]]
        by, to, part = ((0, 1, "all"), (0, -1, "all"), (-1, 1, "lower"), (1, -1, "upper"))[kind]
        offsets = where_of(colour, unit, by)
        where = {name: at(name, v) for name, v in offsets.items()}
        rows = rows_of(colour, part)
        dst = place(where, rows, me["c"])
        i = number[unit]
        return pltpu.make_async_remote_copy(
            src_ref=dst,
            dst_ref=dst,
            send_sem=send_sem.at[colour, i, kind],
            recv_sem=recv_sem.at[colour, i, kind],
            device_id={axis: at(axis, to)},
            device_id_type=MESH,
        )

    def send(colour, unit):
        for kind in (0, 1):
            copy = remote(colour, unit, kind)
            copy.start()
            started.append(copy)

    def arrived(colour, unit):
        for kind in (0, 1):
            remote(colour, unit, kind).wait_recv()
        for kind in (2, 3):
            copy = remote(colour, unit, kind)
            copy.start()
            started.append(copy)

    def arrived_far(colour, unit):
        for kind in (2, 3):
            remote(colour, unit, kind).wait_recv()

    crossings = []

    def cross(colour, second, third):
        axes = ORDERS[colour]
        where = {axes[1]: at(axes[1], second), axes[2]: at(axes[2], third)}
        ref = place(where, rows_of(colour, "all"), me["c"])
        i = ((0, -1, 1, 2).index(second)) * 4 + (0, -1, 1, 2).index(third)
        copy = pltpu.make_async_remote_copy(
            src_ref=ref,
            dst_ref=ref,
            send_sem=sib_send.at[colour, i],
            recv_sem=sib_recv.at[colour, i],
            device_id=other,
            device_id_type=MESH,
        )
        copy.start()
        other_ref = place(where, rows_of(colour, "all"), other["c"])
        arrival = pltpu.make_async_remote_copy(
            src_ref=other_ref,
            dst_ref=other_ref,
            send_sem=sib_send.at[colour, i],
            recv_sem=sib_recv.at[colour, i],
            device_id=other,
            device_id_type=MESH,
        )
        crossings.append((copy, arrival))

    done_leaves = [0]

    def near(count):
        first = done_leaves[0]
        last = min(leaves, first + count)
        done_leaves[0] = last
        if last == first:
            return
        if first == 0:
            for copy in halo:
                copy.wait_recv()

            @pl.when(column == 0)
            def _():
                xbuf[:leaves] = jnp.zeros((leaves,) + xbuf.shape[1:], BF16)

            @pl.when(column == gx - 1)
            def _():
                xbuf[2 * leaves :] = jnp.zeros((leaves,) + xbuf.shape[1:], BF16)

        def body(leaf, carry):
            slot = lax.rem(leaf, depth)
            near_copy(leaf, slot).wait()
            lanes = pl.ds(pl.multiple_of(leaf * panels, panels), panels)
            total = xbuf[leaves + leaf].astype(F32)
            for k in range(slots):
                live = lax.min(lax.max(near_count_ref[leaf] - k, 0), 1).astype(F32)
                total = total + live * dot(xbuf[src_ref[k, leaf]], nbuf[slot, k], NT)
            base_ref[:, lanes] = total

            @pl.when(leaf + depth < leaves)
            def _():
                near_copy(leaf + depth, slot).start()

            return carry

        lax.fori_loop(first, last, body, 0)

    def list_region(stage_index):
        index = [me["x"], me["c"], me["y"], me["z"]]
        for place_of in ((), (0,), (0, 2), (0, 2, 3))[stage_index]:
            index[place_of] = slice(None)
        return lists.at[tuple(index)]

    def list_copies(i):
        if i == 3:
            targets = [other]
        else:
            axis = ("x", "y", "z")[i]
            targets = [{axis: at(axis, by)} for by in (1, 2, 3)]
        region = list_region(i)
        out = []
        for t, target in enumerate(targets):
            out.append(
                pltpu.make_async_remote_copy(
                    src_ref=region, dst_ref=region,
                    send_sem=list_send.at[i, t], recv_sem=list_recv.at[i, t],
                    device_id=target, device_id_type=MESH,
                )
            )
        return out

    list_sent = []

    def lists_go(i):
        for copy in list_copies(i):
            copy.start()
            list_sent.append(copy)

    def lists_come(i):
        for copy in list_copies(i):
            copy.wait_recv()

    colours = range(3)
    keep.wait()
    keep_list.wait()
    lists_go(0)
    for unit in (units[0], (1, 0, None), (2, 0, 0)):
        for k in colours:
            send(k, unit)
    for k in colours:
        arrived(k, units[0])
        for r in (-1, 1):
            send(k, (1, r, None))
    for k in colours:
        arrived_far(k, units[0])
        send(k, (1, 2, None))
    for k in colours:
        arrived(k, (1, 0, None))
        for r in (-1, 1, 2):
            send(k, (2, r, 0))
    for k in colours:
        cross(k, 0, 0)
    lists_come(0)
    lists_go(1)
    for r in (-1, 1, 2):
        for k in colours:
            arrived(k, (1, r, None))
    for k in colours:
        arrived(k, (2, 0, 0))
    for r in (-1, 1):
        for k in colours:
            send(k, (2, None, r))
    for r in (0, -1, 1, 2):
        for k in colours:
            arrived_far(k, (1, r, None))
    for k in colours:
        send(k, (2, None, 2))
    for r in (-1, 1, 2):
        for k in colours:
            cross(k, r, 0)
    lists_come(1)
    lists_go(2)
    near(1)
    for r in (-1, 1, 2):
        for k in colours:
            arrived(k, (2, r, 0))
        near(1)
    lists_come(2)
    lists_go(3)
    for k in colours:
        for t in (-1, 1):
            cross(k, 0, t)
    near(1)
    for r in (-1, 1):
        for k in colours:
            arrived(k, (2, None, r))
            for t in (-1, 1):
                cross(k, r, t)
            near(1)
    for r in (0, -1, 1, 2):
        for k in colours:
            arrived_far(k, (2, r, 0))
        near(1)
    for k in colours:
        cross(k, 0, 2)
    near(leaves)
    lists_come(3)
    index = ((me["x"] * 2 + me["c"]) * 4 + me["y"]) * 4 + me["z"]
    peers_all = lists.shape[-1]
    mark = (lax.broadcasted_iota(jnp.int32, (8, peers_all), 1) == index).astype(BF16)
    table = dot(mark, lists[...].reshape(-1, peers_all).astype(F32).astype(BF16), NT)
    table_ref[...] = table[:1].astype(jnp.int32)
    for k in colours:
        arrived(k, (2, None, 2))
        for t in (-1, 1):
            cross(k, 2, t)
    for r in (-1, 1, 2):
        for k in colours:
            arrived_far(k, (2, None, r))
            cross(k, r, 2)
    for copy, arrival in crossings:
        arrival.wait_recv()
    for copy, arrival in crossings:
        copy.wait_send()
    for copy in started + list_sent:
        copy.wait_send()
    for copy in halo:
        copy.wait_send()


def spread(basis, p2m, near_blocks, send_list, send_count, near_src, near_count):
    leaves, slots, panels, _ = near_blocks.shape
    rhs = basis.shape[1]
    terms = p2m.shape[2]
    rows = leaves * rhs
    peers = send_list.shape[1]
    tiles = rows // 16
    cuts = (0, 22 * 16, 42 * 16, tiles * 16)
    depth = 4
    hbm = pl.BlockSpec(memory_space=pltpu.HBM)
    vmem = pl.BlockSpec(memory_space=pltpu.VMEM)
    smem = pl.BlockSpec(memory_space=pltpu.SMEM)
    dma = pltpu.SemaphoreType.DMA
    return pl.pallas_call(
        functools.partial(spread_kernel, cuts),
        in_specs=[hbm, hbm, hbm, vmem, vmem, smem, smem],
        out_specs=(hbm, vmem, vmem),
        out_shape=(
            jax.ShapeDtypeStruct((4, 2, 4, 4, rows, terms), BF16),
            jax.ShapeDtypeStruct((rhs, leaves * panels), F32),
            jax.ShapeDtypeStruct((1, peers * 8), jnp.int32),
        ),
        scratch_shapes=[
            pltpu.VMEM((3 * leaves, rhs, panels), BF16),
            pltpu.VMEM((depth, slots, panels, panels), BF16),
            pltpu.VMEM((leaves, panels, terms), BF16),
            pltpu.VMEM((rows, terms), BF16),
            pltpu.VMEM((8, peers), jnp.int32),
            pltpu.VMEM((4, 2, 4, 4, 8, peers), jnp.int32),
            dma((3, 12, 4)), dma((3, 12, 4)), dma((3, 16)), dma((3, 16)),
            dma((2,)), dma((2,)), dma((4, 3)), dma((4, 3)),
            dma, dma, dma, dma, dma((depth,)),
        ],
        compiler_params=pltpu.CompilerParams(
            collective_id=0, has_side_effects=True, vmem_limit_bytes=LIMIT
        ),
        name="spread",
    )(
        basis, p2m, near_blocks, jnp.swapaxes(send_list, 1, 2), send_count,
        near_src.T, near_count,
    )


def far_kernel(
    src_ref, class_ref, table_ref, all_ref, base_ref, p_hbm, m2l_hbm, basis_ref,
    image_ref, inner_ref,
    buf, acc_a, acc_b, grouped, vbuf, p_ref, m2l_ref, sems, vsem,
):
    leaves, panels, terms = p_ref.shape
    rhs = base_ref.shape[0]
    slots = src_ref.shape[1]
    classes = m2l_ref.shape[0] // terms
    blocks = basis_ref.shape[0]
    ahead = 4
    group = grouped.shape[0] // rhs

    def fetch(leaf):
        def one(e, carry):
            f = src_ref[leaf, e]
            sender = lax.shift_right_logical(f, 2)
            at = table_ref[0, sender * 8 + (f & 3)]
            rows = pl.ds(pl.multiple_of(at * rhs, rhs), rhs)
            pltpu.make_async_copy(
                all_ref.at[sender, rows], buf.at[leaf * slots + e], sems.at[leaf]
            ).start()
            return carry

        lax.fori_loop(0, slots, one, 0, unroll=8)

    loads = [
        pltpu.make_async_copy(a, b, vsem.at[i])
        for i, (a, b) in enumerate(((m2l_hbm, m2l_ref), (p_hbm, p_ref), (basis_ref, vbuf)))
    ]
    for leaf in range(ahead):
        fetch(leaf)
    for load in loads:
        load.start()
    inner_ref[...] = jnp.zeros_like(inner_ref)

    def per_group(g, carry):
        def per_pair(j, carry):
            first = g * group + j * 2

            @pl.when(first + ahead < leaves)
            def _():
                fetch(first + ahead)
                fetch(first + ahead + 1)

            for by in range(2):
                view = buf.at[pl.ds((first + by) * slots, slots)]
                pltpu.make_async_copy(view, view, sems.at[first + by]).wait()
            acc_a[...] = jnp.zeros_like(acc_a)
            acc_b[...] = jnp.zeros_like(acc_b)

            def one(e, carry):
                for acc, leaf in ((acc_a, first), (acc_b, first + 1)):
                    f = src_ref[leaf, e]
                    sender = lax.shift_right_logical(f, 2)
                    valid = (f & 3) < table_ref[0, sender * 8 + 4]
                    which = jnp.where(valid, class_ref[leaf, e], classes)
                    acc[which] += buf[leaf * slots + e].astype(F32)
                return carry

            lax.fori_loop(0, slots, one, 0, unroll=4)
            for by, acc in ((0, acc_a), (1, acc_b)):
                at = pl.ds(pl.multiple_of((j * 2 + by) * rhs, rhs), rhs)
                for c in range(classes):
                    grouped[at, c * terms : (c + 1) * terms] = acc[c].astype(BF16)
            return carry

        lax.fori_loop(0, group // 2, per_pair, 0)

        @pl.when(g == 0)
        def _():
            for load in loads:
                load.wait()

        local = dot(grouped[...], m2l_ref[...]).astype(BF16)

        for j in range(group):
            leaf = g * group + j
            lanes = pl.ds(pl.multiple_of(leaf * panels, panels), panels)
            far = dot(local[j * rhs : (j + 1) * rhs], p_ref[leaf], NT)
            image = base_ref[:, lanes] + far
            image_ref[:, lanes] = image
            both = jnp.concatenate(halves(image), axis=0)
            v = vbuf[:, :, lanes].reshape(blocks * rhs, panels)
            out = dot(both, v, NT)
            inner_ref[...] += out[:rhs] + out[rhs:]
        return carry

    lax.fori_loop(0, leaves // group, per_group, 0)


def far_field(far_src, far_class, table, everyone, base, p2m, m2l, basis):
    leaves, panels, terms = p2m.shape
    blocks, rhs, columns = basis.shape
    slots = far_src.shape[1]
    classes = m2l.shape[0]
    hbm = pl.BlockSpec(memory_space=pltpu.HBM)
    vmem = pl.BlockSpec(memory_space=pltpu.VMEM)
    smem = pl.BlockSpec(memory_space=pltpu.SMEM)
    dma = pltpu.SemaphoreType.DMA
    group = 4
    return pl.pallas_call(
        far_kernel,
        in_specs=[smem, smem, smem, hbm, vmem, hbm, hbm, hbm],
        out_specs=(vmem, vmem),
        out_shape=(
            jax.ShapeDtypeStruct((rhs, columns), F32),
            jax.ShapeDtypeStruct((rhs, blocks * rhs), F32),
        ),
        scratch_shapes=[
            pltpu.VMEM((leaves * slots, rhs, terms), BF16),
            pltpu.VMEM((classes + 1, rhs, terms), F32),
            pltpu.VMEM((classes + 1, rhs, terms), F32),
            pltpu.VMEM((group * rhs, classes * terms), BF16),
            pltpu.VMEM((blocks, rhs, columns), BF16),
            pltpu.VMEM((leaves, panels, terms), BF16),
            pltpu.VMEM((classes * terms, terms), BF16),
            dma((leaves,)), dma((3,)),
        ],
        compiler_params=pltpu.CompilerParams(vmem_limit_bytes=LIMIT),
        name="far_field",
    )(
        far_src, far_class, table, everyone, base, p2m,
        m2l.reshape(classes * terms, terms), basis,
    )


def finish_kernel(
    total_rows, inner_ref, image_ref, basis_ref,
    next_ref, proj_ref, factor_ref,
    vbuf, image, gram_in, one_in, two_in, stack, piece, whole, gone, narrow, two_gone,
    s1, r1, s2, r2, s3, r3, vsem, isem,
):
    me = {name: lax.axis_index(name) for name in ALL}
    column = me["x"] * 2 + me["c"]
    gx = 8
    rhs, columns = image_ref.shape
    blocks = basis_ref.shape[0]
    load = pltpu.make_async_copy(basis_ref, vbuf, vsem)
    load.start()
    load_image = pltpu.make_async_copy(image_ref, image, isem)
    load_image.start()

    def col_peer(by):
        c = lax.rem(column + by, gx)
        return c, {"x": c // 2, "c": lax.rem(c, 2)}

    def line_peer(axis, by):
        c = lax.rem(me[axis] + by, 4)
        return c, {axis: c}

    barrier = pltpu.get_barrier_semaphore()
    for by in range(1, gx):
        pl.semaphore_signal(barrier, inc=1, device_id=col_peer(by)[1], device_id_type=MESH)
    for axis in ("y", "z"):
        for by in range(1, 4):
            peer = line_peer(axis, by)[1]
            pl.semaphore_signal(barrier, inc=1, device_id=peer, device_id_type=MESH)
    pl.semaphore_wait(barrier, gx - 1 + 6)

    def remote(src, dst, send, recv, peer):
        return pltpu.make_async_remote_copy(
            src_ref=src, dst_ref=dst, send_sem=send, recv_sem=recv,
            device_id=peer, device_id_type=MESH,
        )

    def all_reduce(n, source, arrivals, mine, parts, result):
        rows = rhs // gx
        sent = []
        for by in range(1, gx):
            c, peer = col_peer(by)
            at = pl.ds(pl.multiple_of(c * rows, rows), rows)
            copy = remote(source.at[at], arrivals.at[gx - by], s1.at[n, by], r1.at[n, gx - by], peer)
            copy.start()
            sent.append(copy)
        own = pl.ds(pl.multiple_of(column * rows, rows), rows)
        total = source[own, :]
        for by in range(1, gx):
            remote(arrivals.at[by], arrivals.at[by], s1.at[n, by], r1.at[n, by], col_peer(1)[1]).wait_recv()
            total = total + arrivals[by]
        for n_axis, axis in enumerate(("y", "z")):
            slot = mine.at[n_axis]
            slot[...] = total
            for by in range(1, 4):
                i = n_axis * 4 + by
                copy = remote(
                    slot, parts.at[n_axis * 4 + me[axis]],
                    s2.at[n, i], r2.at[n, n_axis * 4 + 4 - by], line_peer(axis, by)[1],
                )
                copy.start()
                sent.append(copy)
            parts[n_axis * 4 + me[axis]] = total
            for by in range(1, 4):
                c, peer = line_peer(axis, by)
                i = n_axis * 4 + by
                remote(slot, parts.at[n_axis * 4 + c], s2.at[n, i], r2.at[n, i], peer).wait_recv()
            total = parts[n_axis * 4]
            for c in range(1, 4):
                total = total + parts[n_axis * 4 + c]
        result[own, :] = total
        for by in range(1, gx):
            c, peer = col_peer(by)
            copy = remote(result.at[own], result.at[own], s3.at[n, by], r3.at[n, gx - by], peer)
            copy.start()
            sent.append(copy)
        for by in range(1, gx):
            c, peer = col_peer(by)
            at = pl.ds(pl.multiple_of(c * rows, rows), rows)
            remote(result.at[at], result.at[at], s3.at[n, by], r3.at[n, by], peer).wait_recv()
        for copy in sent:
            copy.wait_send()

    scale = 1.0 / total_rows
    all_reduce(0, inner_ref, one_in, piece, two_in, whole)
    load.wait()
    load_image.wait()
    proj = whole[...] * scale
    coef = jnp.concatenate(halves(proj), axis=0)
    step = 512
    gram = jnp.zeros((2 * rhs, 2 * rhs), F32)
    for i in range(0, columns, step):
        v = vbuf[:, :, i : i + step].reshape(blocks * rhs, step)
        out = dot(coef, v)
        resid = image[:, i : i + step] - (out[:rhs] + out[rhs:])
        both = jnp.concatenate(halves(resid), axis=0)
        stack[:, i : i + step] = both
        gram = gram + dot(both, both, NT)
    gram_in[...] = gram[:rhs] + gram[rhs:]
    for i in range(0, blocks * rhs, 2 * rhs):
        proj_ref[i : i + 2 * rhs, :] = proj[:, i : i + 2 * rhs].T
    all_reduce(1, gram_in, gone, narrow, two_gone, factor_ref)
    folded = factor_ref[...] * scale
    folded = folded + pltpu.roll(folded, rhs, 1)
    lane = lax.broadcasted_iota(jnp.int32, (rhs, 2 * rhs), 1)
    row = lax.broadcasted_iota(jnp.int32, (rhs, 2 * rhs), 0)
    work = jnp.where(lane < rhs, folded, (lane - rhs == row).astype(F32))
    tall = 8
    count = rhs // tall
    part = [work[i * tall : (i + 1) * tall] for i in range(count)]
    low = lax.broadcasted_iota(jnp.int32, (tall, 2 * rhs), 0)
    for b in range(count):
        cols = [
            {i: jnp.broadcast_to(part[i][:, b * tall + t : b * tall + t + 1], (tall, 2 * rhs)) for i in range(b, count)}
            for t in range(tall)
        ]
        for t in range(tall):
            inverse = 1.0 / cols[t][b][t : t + 1, :]
            across = {u: cols[u][b][t : t + 1, :] * inverse for u in range(t + 1, tall)}
            pivot = part[b][t : t + 1, :] * inverse
            for i in range(b, count):
                factor = cols[t][i]
                if i == b:
                    factor = jnp.where(low > t, factor, 0.0)
                part[i] = part[i] - factor * pivot
                for u in range(t + 1, tall):
                    cols[u][i] = cols[u][i] - factor * across[u]
    work = jnp.concatenate(part, axis=0)
    diagonal = jnp.sum(jnp.where(lane == row, work, 0.0), axis=1, keepdims=True)
    work = work * lax.rsqrt(diagonal)
    factor_ref[...] = jnp.where((lane >= row) & (lane < rhs), work, 0.0)
    right = jnp.where(lane < rhs, 0.0, work)
    right = right + pltpu.roll(right, rhs, 1)
    left = jnp.concatenate(halves(right), axis=0)
    for i in range(0, columns, step):
        out = dot(left, stack[:, i : i + step])
        next_ref[:, i : i + step] = (out[:rhs] + out[rhs:]).astype(BF16)


def finish(inner, image, basis, total_rows):
    blocks, rhs, columns = basis.shape
    wide = blocks * rhs
    hbm = pl.BlockSpec(memory_space=pltpu.HBM)
    vmem = pl.BlockSpec(memory_space=pltpu.VMEM)
    dma = pltpu.SemaphoreType.DMA
    return pl.pallas_call(
        functools.partial(finish_kernel, total_rows),
        in_specs=[vmem, hbm, hbm],
        out_specs=(vmem, vmem, vmem),
        out_shape=(
            jax.ShapeDtypeStruct((rhs, columns), BF16),
            jax.ShapeDtypeStruct((wide, rhs), F32),
            jax.ShapeDtypeStruct((rhs, 2 * rhs), F32),
        ),
        scratch_shapes=[
            pltpu.VMEM((blocks, rhs, columns), BF16),
            pltpu.VMEM((rhs, columns), F32),
            pltpu.VMEM((rhs, 2 * rhs), F32),
            pltpu.VMEM((8, 8, wide), F32),
            pltpu.VMEM((8, 8, wide), F32),
            pltpu.VMEM((2 * rhs, columns), BF16),
            pltpu.VMEM((2, 8, wide), F32),
            pltpu.VMEM((rhs, wide), F32),
            pltpu.VMEM((8, 8, 2 * rhs), F32),
            pltpu.VMEM((2, 8, 2 * rhs), F32),
            pltpu.VMEM((8, 8, 2 * rhs), F32),
            dma((2, 8)), dma((2, 8)), dma((2, 8)), dma((2, 8)), dma((2, 8)), dma((2, 8)), dma, dma,
        ],
        compiler_params=pltpu.CompilerParams(
            collective_id=1, has_side_effects=True, vmem_limit_bytes=LIMIT
        ),
        name="finish",
    )(inner, image, basis)


def shards(
    basis, near_blocks, near_src, near_count, p2m, m2l, send_list, send_count, far_src, far_class
):
    blocks, rhs, columns = basis.shape
    leaves, panels, terms = p2m.shape
    peers = lax.axis_size(ALL)
    everyone, base, table = spread(
        basis, p2m, near_blocks, send_list, send_count, near_src, near_count
    )
    everyone = everyone.reshape(peers, leaves * rhs, terms)
    image, inner = far_field(far_src, far_class, table, everyone, base, p2m, m2l, basis)
    new, proj, upper = finish(inner, image, basis, columns * peers)
    factor = upper[:, :rhs].T
    return (new, proj.reshape(blocks, rhs, rhs), factor)


def solution(mesh):
    finer = Mesh(mesh.devices.reshape(4, 2, 4, 4), ALL)
    in_specs = (
        P(None, None, ALL),
        P(ALL, None, None, None),
        P(ALL, None),
        P(ALL),
        P(ALL, None, None),
        P(),
        P(ALL, None, None),
        P(ALL, None),
        P(ALL, None),
        P(ALL, None),
    )
    out_specs = (P(None, ALL), P(), P())
    return jax.shard_map(
        shards, mesh=finer, in_specs=in_specs, out_specs=out_specs, check_vma=False
    )
```

```python
import functools

import jax
import jax.numpy as jnp
from jax import lax
from jax.experimental import pallas as pl
from jax.experimental.pallas import tpu as pltpu
from jax.sharding import Mesh
from jax.sharding import PartitionSpec as P

ALL = ("x", "c", "y", "z")
ORDERS = (("x", "y", "z"), ("y", "z", "x"), ("z", "x", "y"))
MESH = pl.DeviceIdType.MESH
F32, BF16 = jnp.float32, jnp.bfloat16
LIMIT = 67043328
NT = (((1,), (1,)), ((), ()))
TN = (((0,), (0,)), ((), ()))


def dot(a, b, dims=(((1,), (0,)), ((), ()))):
    return lax.dot_general(a, b, dims, preferred_element_type=F32)


def halves(values):
    upper = values.astype(BF16)
    return upper, (values - upper.astype(F32)).astype(BF16)


def step_kernel(
    cuts, total_rows, basis_ref, p_ref, near_blocks_ref, m2l_ref, list_ref, count_ref,
    src_ref, near_count_ref, far_ref, class_ref,
    next_ref, proj_ref, factor_ref,
    all_ref, xbuf, nbuf, pbuf, mbuf, stage, lists, base_ref, vbuf, mats, table_ref, table,
    inner_ref, gram_in, one_in, two_in, stack, piece, whole, gone, narrow, two_gone, gram_out,
    s1, r1, s2, r2, s3, r3, v_sem, m_sem, t_sem,
    send_sem, recv_sem, sib_send, sib_recv, halo_send, halo_recv, list_send, list_recv,
    own_sem, x_sem, p_sem, stage_sem, nsem,
):
    me = {name: lax.axis_index(name) for name in ALL}
    leaves = near_blocks_ref.shape[0]
    slots = near_blocks_ref.shape[1]
    panels = near_blocks_ref.shape[2]
    depth = nbuf.shape[0]
    column = me["x"] * 2 + me["c"]

    def at(axis, by):
        return lax.rem(me[axis] + (by + 4), 4)

    def near_copy(leaf, slot):
        return pltpu.make_async_copy(near_blocks_ref.at[leaf], nbuf.at[slot], nsem.at[slot])

    blocks, rhs = basis_ref.shape[:2]
    mine = xbuf.at[pl.ds(leaves, leaves)]
    for leaf in range(leaves):
        pltpu.make_async_copy(
            basis_ref.at[blocks - 1, :, pl.ds(leaf * panels, panels)], mine.at[leaf], x_sem
        ).start()
    load_p = pltpu.make_async_copy(p_ref, pbuf, p_sem)
    load_p.start()
    load_v = pltpu.make_async_copy(basis_ref, vbuf, v_sem)
    load_v.start()
    classes, terms = m2l_ref.shape[:2]
    load_m = pltpu.make_async_copy(m2l_ref, mats.at[pl.ds(0, classes)], m_sem)
    load_m.start()
    mats[classes] = jnp.zeros((terms, terms), BF16)
    for leaf in range(depth):
        near_copy(leaf, leaf).start()

    other = {"c": 1 - me["c"]}
    barrier = pltpu.get_barrier_semaphore()
    gx = 8

    def col_peer(by):
        c = lax.rem(column + by, gx)
        return c, {"x": c // 2, "c": lax.rem(c, 2)}

    def line_peer(axis, by):
        c = lax.rem(me[axis] + by, 4)
        return c, {axis: c}

    after, before = col_peer(1)[1], col_peer(gx - 1)[1]
    peers = [col_peer(by)[1] for by in range(1, gx)]
    peers += [line_peer(axis, by)[1] for axis in ("y", "z") for by in range(1, 4)]
    for peer in peers:
        pl.semaphore_signal(barrier, inc=1, device_id=peer, device_id_type=MESH)
    slots_out = list_ref.shape[1]
    stage[...] = jnp.zeros_like(stage)
    stage[:slots_out, :] = list_ref[0]
    stage[slots_out : slots_out + 1, :] = count_ref[...]
    def list_region(stage_index):
        index = [me["x"], me["c"], me["y"], me["z"]]
        for place_of in ((), (0,), (0, 2), (0, 2, 3))[stage_index]:
            index[place_of] = slice(None)
        return lists.at[tuple(index)]

    def list_copies(i):
        if i == 3:
            targets = [other]
        else:
            axis = ("x", "y", "z")[i]
            targets = [{axis: at(axis, by)} for by in (1, 2, 3)]
        region = list_region(i)
        out = []
        for t, target in enumerate(targets):
            out.append(
                pltpu.make_async_remote_copy(
                    src_ref=region, dst_ref=region,
                    send_sem=list_send.at[i, t], recv_sem=list_recv.at[i, t],
                    device_id=target, device_id_type=MESH,
                )
            )
        return out

    list_sent = []

    def lists_go(i):
        for copy in list_copies(i):
            copy.start()
            list_sent.append(copy)

    def lists_come(i):
        for copy in list_copies(i):
            copy.wait_recv()

    my_list = lists.at[me["x"], me["c"], me["y"], me["z"]]
    keep_list = pltpu.make_async_copy(stage, my_list, stage_sem)
    keep_list.start()
    pltpu.make_async_copy(mine, mine, x_sem).wait()
    load_p.wait()
    keep_list.wait()
    pl.semaphore_wait(barrier, len(peers))
    lists_go(0)

    def multipole(leaf, carry):
        block = dot(xbuf[leaves + leaf], pbuf[leaf]).astype(BF16)
        mbuf[2 * leaf] = block[: rhs // 2]
        mbuf[2 * leaf + 1] = block[rhs // 2 :]
        return carry

    lax.fori_loop(0, leaves, multipole, 0, unroll=4)
    here = all_ref.at[me["x"], me["c"], me["y"], me["z"]]
    keep = pltpu.make_async_copy(mbuf, here, own_sem)
    keep.start()

    def place(where, rows, core):
        index = []
        for name in ALL:
            if name == "c":
                index.append(core)
            elif name in where:
                index.append(where[name])
            else:
                index.append(slice(None))
        return all_ref.at[tuple(index) + (pl.ds(rows[0], rows[1] - rows[0]),)]

    units = [(0, None, None)]
    units += [(1, r, None) for r in (0, -1, 1, 2)]
    units += [(2, r, 0) for r in (0, -1, 1, 2)]
    units += [(2, None, r) for r in (-1, 1, 2)]
    number = {u: i for i, u in enumerate(units)}
    started = []

    def where_of(colour, unit, by):
        axes = ORDERS[colour]
        phase, first, second = unit
        where = {}
        if phase == 0:
            where = {axes[0]: by, axes[1]: 0, axes[2]: 0}
        elif phase == 1:
            where = {axes[0]: first, axes[1]: by, axes[2]: 0}
        else:
            where = {axes[1]: second, axes[2]: by}
            if first is not None:
                where[axes[0]] = first
        return where

    def rows_of(colour, part):
        low, high = cuts[colour], cuts[colour + 1]
        middle = low + (high - low) // 2
        return {"all": (low, high), "lower": (low, middle), "upper": (middle, high)}[part]

    def remote(colour, unit, kind):
        axis = ORDERS[colour][unit[0]]
        by, to, part = ((0, 1, "all"), (0, -1, "all"), (-1, 1, "lower"), (1, -1, "upper"))[kind]
        offsets = where_of(colour, unit, by)
        where = {name: at(name, v) for name, v in offsets.items()}
        rows = rows_of(colour, part)
        dst = place(where, rows, me["c"])
        i = number[unit]
        return pltpu.make_async_remote_copy(
            src_ref=dst,
            dst_ref=dst,
            send_sem=send_sem.at[colour, i, kind],
            recv_sem=recv_sem.at[colour, i, kind],
            device_id={axis: at(axis, to)},
            device_id_type=MESH,
        )

    def send(colour, unit):
        for kind in (0, 1):
            copy = remote(colour, unit, kind)
            copy.start()
            started.append(copy)

    def arrived(colour, unit):
        for kind in (0, 1):
            remote(colour, unit, kind).wait_recv()
        for kind in (2, 3):
            copy = remote(colour, unit, kind)
            copy.start()
            started.append(copy)

    def arrived_far(colour, unit):
        for kind in (2, 3):
            remote(colour, unit, kind).wait_recv()

    crossings = []

    def cross(colour, second, third):
        axes = ORDERS[colour]
        where = {axes[1]: at(axes[1], second), axes[2]: at(axes[2], third)}
        ref = place(where, rows_of(colour, "all"), me["c"])
        i = ((0, -1, 1, 2).index(second)) * 4 + (0, -1, 1, 2).index(third)
        copy = pltpu.make_async_remote_copy(
            src_ref=ref,
            dst_ref=ref,
            send_sem=sib_send.at[colour, i],
            recv_sem=sib_recv.at[colour, i],
            device_id=other,
            device_id_type=MESH,
        )
        copy.start()
        other_ref = place(where, rows_of(colour, "all"), other["c"])
        arrival = pltpu.make_async_remote_copy(
            src_ref=other_ref,
            dst_ref=other_ref,
            send_sem=sib_send.at[colour, i],
            recv_sem=sib_recv.at[colour, i],
            device_id=other,
            device_id_type=MESH,
        )
        crossings.append((copy, arrival))

    done_leaves = [0]

    def near(count):
        first = done_leaves[0]
        last = min(leaves, first + count)
        done_leaves[0] = last
        if last == first:
            return
        if first == 0:
            for copy in halo:
                copy.wait_recv()

            @pl.when(column == 0)
            def _():
                xbuf[:leaves] = jnp.zeros((leaves,) + xbuf.shape[1:], BF16)

            @pl.when(column == gx - 1)
            def _():
                xbuf[2 * leaves :] = jnp.zeros((leaves,) + xbuf.shape[1:], BF16)

        def body(leaf, carry):
            slot = lax.rem(leaf, depth)
            near_copy(leaf, slot).wait()
            lanes = pl.ds(pl.multiple_of(leaf * panels, panels), panels)
            total = xbuf[leaves + leaf].astype(F32)
            for k in range(slots):
                live = lax.min(lax.max(near_count_ref[leaf] - k, 0), 1).astype(F32)
                total = total + live * dot(xbuf[src_ref[k, leaf]], nbuf[slot, k], NT)
            base_ref[:, lanes] = total

            @pl.when(leaf + depth < leaves)
            def _():
                near_copy(leaf + depth, slot).start()

            return carry

        lax.fori_loop(first, last, body, 0)

    colours = range(3)
    keep.wait()
    for k in colours:
        send(k, units[0])
    lists_come(0)
    lists_go(1)
    for k in colours:
        send(k, (1, 0, None))
    for k in colours:
        arrived(k, units[0])
        for r in (-1, 1):
            send(k, (1, r, None))
    lists_come(1)
    lists_go(2)
    for k in colours:
        arrived_far(k, units[0])
        send(k, (1, 2, None))
    for k in colours:
        send(k, (2, 0, 0))
    for k in colours:
        arrived(k, (1, 0, None))
        for r in (-1, 1, 2):
            send(k, (2, r, 0))
    for k in colours:
        cross(k, 0, 0)
    for r in (-1, 1, 2):
        for k in colours:
            arrived(k, (1, r, None))
    for k in colours:
        arrived(k, (2, 0, 0))
    for r in (-1, 1):
        for k in colours:
            send(k, (2, None, r))
    halo = []
    for i, (target, slot) in enumerate(((after, 0), (before, 2))):
        copy = pltpu.make_async_remote_copy(
            src_ref=mine,
            dst_ref=xbuf.at[pl.ds(slot * leaves, leaves)],
            send_sem=halo_send.at[i],
            recv_sem=halo_recv.at[i],
            device_id=target,
            device_id_type=MESH,
        )
        copy.start()
        halo.append(copy)
    for r in (0, -1, 1, 2):
        for k in colours:
            arrived_far(k, (1, r, None))
    for k in colours:
        send(k, (2, None, 2))
    for r in (-1, 1, 2):
        for k in colours:
            cross(k, r, 0)
    lists_come(2)
    lists_go(3)
    for r in (-1, 1, 2):
        for k in colours:
            arrived(k, (2, r, 0))
    for k in colours:
        for t in (-1, 1):
            cross(k, 0, t)
    for r in (-1, 1):
        for k in colours:
            arrived(k, (2, None, r))
            for t in (-1, 1):
                cross(k, r, t)
            if r == 1:
                near(2)
    for r in (0, -1, 1, 2):
        for k in colours:
            arrived_far(k, (2, r, 0))
        near(2)
    for k in colours:
        cross(k, 0, 2)
    near(leaves)
    lists_come(3)
    index = ((me["x"] * 2 + me["c"]) * 4 + me["y"]) * 4 + me["z"]
    peers_all = lists.shape[-1]
    mark = (lax.broadcasted_iota(jnp.int32, (8, peers_all), 1) == index).astype(BF16)
    picked = dot(mark, lists[...].reshape(-1, peers_all).astype(F32).astype(BF16), NT)
    table_ref[...] = picked[:1].astype(jnp.int32)
    to_scalar = pltpu.make_async_copy(table_ref, table, t_sem)
    to_scalar.start()
    for k in colours:
        arrived(k, (2, None, 2))
        for t in (-1, 1):
            cross(k, 2, t)
    for r in (-1, 1, 2):
        for k in colours:
            arrived_far(k, (2, None, r))
            cross(k, r, 2)
    for copy, arrival in crossings:
        arrival.wait_recv()
    to_scalar.wait()
    load_m.wait()
    load_v.wait()
    far_slots = far_ref.shape[1]
    inner_ref[...] = jnp.zeros_like(inner_ref)

    def far(leaf, carry):
        total = jnp.zeros((rhs, terms), F32)
        for pair in range(far_slots // 2):
            sources, steps = [], []
            for e in (2 * pair, 2 * pair + 1):
                f = far_ref[leaf, e]
                sender = lax.shift_right_logical(f, 2)
                slot = f & 3
                unit = lax.min(lax.max(table[0, sender * 8 + slot], 0), leaves - 1) * 2
                live = lax.min(lax.max(table[0, sender * 8 + 4] - slot, 0), 1)
                which = classes - live * (classes - class_ref[leaf, e])
                place_x = lax.shift_right_logical(sender, 5)
                place_c = lax.shift_right_logical(sender, 4) & 1
                place_y = lax.shift_right_logical(sender, 2) & 3
                place_z = sender & 3
                sources.append(
                    jnp.concatenate(
                        [
                            all_ref[place_x, place_c, place_y, place_z, unit],
                            all_ref[place_x, place_c, place_y, place_z, unit + 1],
                        ],
                        axis=0,
                    )
                )
                steps.append(mats[which])
            total = total + dot(
                jnp.concatenate(sources, axis=1), jnp.concatenate(steps, axis=0)
            )
        lanes = pl.ds(pl.multiple_of(leaf * panels, panels), panels)
        image = base_ref[:, lanes] + dot(total.astype(BF16), pbuf[leaf], NT)
        base_ref[:, lanes] = image
        both = jnp.concatenate(halves(image), axis=0)
        out = dot(both, vbuf[:, :, lanes].reshape(blocks * rhs, panels), NT)
        inner_ref[...] += out[:rhs] + out[rhs:]
        return carry

    lax.fori_loop(0, leaves, far, 0)
    columns = leaves * panels
    def send_to(src, dst, send, recv, peer):
        return pltpu.make_async_remote_copy(
            src_ref=src, dst_ref=dst, send_sem=send, recv_sem=recv,
            device_id=peer, device_id_type=MESH,
        )

    def all_reduce(n, source, arrivals, mine, parts, result):
        rows = rhs // gx
        sent = []
        for by in range(1, gx):
            c, peer = col_peer(by)
            at = pl.ds(pl.multiple_of(c * rows, rows), rows)
            copy = send_to(source.at[at], arrivals.at[gx - by], s1.at[n, by], r1.at[n, gx - by], peer)
            copy.start()
            sent.append(copy)
        own = pl.ds(pl.multiple_of(column * rows, rows), rows)
        total = source[own, :]
        for by in range(1, gx):
            send_to(arrivals.at[by], arrivals.at[by], s1.at[n, by], r1.at[n, by], col_peer(1)[1]).wait_recv()
            total = total + arrivals[by]
        for n_axis, axis in enumerate(("y", "z")):
            slot = mine.at[n_axis]
            slot[...] = total
            for by in range(1, 4):
                i = n_axis * 4 + by
                copy = send_to(
                    slot, parts.at[n_axis * 4 + me[axis]],
                    s2.at[n, i], r2.at[n, n_axis * 4 + 4 - by], line_peer(axis, by)[1],
                )
                copy.start()
                sent.append(copy)
            parts[n_axis * 4 + me[axis]] = total
            for by in range(1, 4):
                c, peer = line_peer(axis, by)
                i = n_axis * 4 + by
                send_to(slot, parts.at[n_axis * 4 + c], s2.at[n, i], r2.at[n, i], peer).wait_recv()
            total = parts[n_axis * 4]
            for c in range(1, 4):
                total = total + parts[n_axis * 4 + c]
        result[own, :] = total
        for by in range(1, gx):
            c, peer = col_peer(by)
            copy = send_to(result.at[own], result.at[own], s3.at[n, by], r3.at[n, gx - by], peer)
            copy.start()
            sent.append(copy)
        for by in range(1, gx):
            c, peer = col_peer(by)
            at = pl.ds(pl.multiple_of(c * rows, rows), rows)
            send_to(result.at[at], result.at[at], s3.at[n, by], r3.at[n, by], peer).wait_recv()
        for copy in sent:
            copy.wait_send()

    scale = 1.0 / total_rows
    all_reduce(0, inner_ref, one_in, piece, two_in, whole)
    proj = whole[...] * scale
    coef = jnp.concatenate(halves(proj), axis=0)
    step = 512
    gram = jnp.zeros((2 * rhs, 2 * rhs), F32)
    for i in range(0, columns, step):
        v = vbuf[:, :, i : i + step].reshape(blocks * rhs, step)
        out = dot(coef, v)
        resid = base_ref[:, i : i + step] - (out[:rhs] + out[rhs:])
        both = jnp.concatenate(halves(resid), axis=0)
        stack[:, i : i + step] = both
        gram = gram + dot(both, both, NT)
    gram_in[...] = gram[:rhs] + gram[rhs:]
    for i in range(0, blocks * rhs, 2 * rhs):
        proj_ref[i : i + 2 * rhs, :] = proj[:, i : i + 2 * rhs].T
    all_reduce(1, gram_in, gone, narrow, two_gone, gram_out)
    folded = gram_out[...] * scale
    folded = folded + pltpu.roll(folded, rhs, 1)
    lane = lax.broadcasted_iota(jnp.int32, (rhs, 2 * rhs), 1)
    row = lax.broadcasted_iota(jnp.int32, (rhs, 2 * rhs), 0)
    work = jnp.where(lane < rhs, folded, (lane - rhs == row).astype(F32))
    tall = 8
    count = rhs // tall
    part = [work[i * tall : (i + 1) * tall] for i in range(count)]
    low = lax.broadcasted_iota(jnp.int32, (tall, 2 * rhs), 0)
    for b in range(count):
        cols = [
            {i: jnp.broadcast_to(part[i][:, b * tall + t : b * tall + t + 1], (tall, 2 * rhs)) for i in range(b, count)}
            for t in range(tall)
        ]
        for t in range(tall):
            inverse = 1.0 / cols[t][b][t : t + 1, :]
            across = {u: cols[u][b][t : t + 1, :] * inverse for u in range(t + 1, tall)}
            pivot = part[b][t : t + 1, :] * inverse
            for i in range(b, count):
                factor = cols[t][i]
                if i == b:
                    factor = jnp.where(low > t, factor, 0.0)
                part[i] = part[i] - factor * pivot
                for u in range(t + 1, tall):
                    cols[u][i] = cols[u][i] - factor * across[u]
    work = jnp.concatenate(part, axis=0)
    diagonal = jnp.sum(jnp.where(lane == row, work, 0.0), axis=1, keepdims=True)
    work = work * lax.rsqrt(diagonal)
    factor_ref[...] = jnp.where((lane >= row) & (lane < rhs), work, 0.0).T[:rhs]
    right = jnp.where(lane < rhs, 0.0, work)
    right = right + pltpu.roll(right, rhs, 1)
    left = jnp.concatenate(halves(right), axis=0)
    for i in range(0, columns, step):
        out = dot(left, stack[:, i : i + step])
        next_ref[:, i : i + step] = (out[:rhs] + out[rhs:]).astype(BF16)
    for copy, arrival in crossings:
        copy.wait_send()
    for copy in started + list_sent:
        copy.wait_send()
    for copy in halo:
        copy.wait_send()


def step(basis, p2m, near_blocks, m2l, send_list, send_count, near_src, near_count, far_src, far_class):
    leaves, slots, panels, _ = near_blocks.shape
    blocks, rhs, columns = basis.shape
    classes, terms = m2l.shape[:2]
    peers = send_list.shape[1]
    units = 2 * leaves
    wide = blocks * rhs
    cuts = (0, 11, 21, units)
    depth = 4
    hbm = pl.BlockSpec(memory_space=pltpu.HBM)
    vmem = pl.BlockSpec(memory_space=pltpu.VMEM)
    smem = pl.BlockSpec(memory_space=pltpu.SMEM)
    dma = pltpu.SemaphoreType.DMA
    return pl.pallas_call(
        functools.partial(step_kernel, cuts, columns * peers),
        in_specs=[hbm, hbm, hbm, hbm, vmem, vmem, smem, smem, smem, smem],
        out_specs=(vmem, vmem, vmem),
        out_shape=(
            jax.ShapeDtypeStruct((rhs, columns), BF16),
            jax.ShapeDtypeStruct((wide, rhs), F32),
            jax.ShapeDtypeStruct((rhs, rhs), F32),
        ),
        scratch_shapes=[
            pltpu.VMEM((4, 2, 4, 4, units, rhs // 2, terms), BF16),
            pltpu.VMEM((3 * leaves, rhs, panels), BF16),
            pltpu.VMEM((depth, slots, panels, panels), BF16),
            pltpu.VMEM((leaves, panels, terms), BF16),
            pltpu.VMEM((units, rhs // 2, terms), BF16),
            pltpu.VMEM((8, peers), jnp.int32),
            pltpu.VMEM((4, 2, 4, 4, 8, peers), jnp.int32),
            pltpu.VMEM((rhs, columns), F32),
            pltpu.VMEM((blocks, rhs, columns), BF16),
            pltpu.VMEM((classes + 1, terms, terms), BF16),
            pltpu.VMEM((1, peers * 8), jnp.int32),
            pltpu.SMEM((1, peers * 8), jnp.int32),
            pltpu.VMEM((rhs, wide), F32),
            pltpu.VMEM((rhs, 2 * rhs), F32),
            pltpu.VMEM((8, 8, wide), F32),
            pltpu.VMEM((8, 8, wide), F32),
            pltpu.VMEM((2 * rhs, columns), BF16),
            pltpu.VMEM((2, 8, wide), F32),
            pltpu.VMEM((rhs, wide), F32),
            pltpu.VMEM((8, 8, 2 * rhs), F32),
            pltpu.VMEM((2, 8, 2 * rhs), F32),
            pltpu.VMEM((8, 8, 2 * rhs), F32),
            pltpu.VMEM((rhs, 2 * rhs), F32),
            dma((2, 8)), dma((2, 8)), dma((2, 8)), dma((2, 8)), dma((2, 8)), dma((2, 8)),
            dma, dma, dma,
            dma((3, 12, 4)), dma((3, 12, 4)), dma((3, 16)), dma((3, 16)),
            dma((2,)), dma((2,)), dma((4, 3)), dma((4, 3)),
            dma, dma, dma, dma, dma((depth,)),
        ],
        compiler_params=pltpu.CompilerParams(
            collective_id=0, has_side_effects=True, vmem_limit_bytes=LIMIT - (896 << 10)
        ),
        name="step",
    )(
        basis, p2m, near_blocks, m2l, jnp.swapaxes(send_list, 1, 2), send_count,
        near_src.T, near_count, far_src, far_class,
    )


def shards(
    basis, near_blocks, near_src, near_count, p2m, m2l, send_list, send_count, far_src, far_class
):
    blocks, rhs, columns = basis.shape
    new, proj, factor = step(
        basis, p2m, near_blocks, m2l, send_list, send_count, near_src, near_count, far_src, far_class
    )
    return (new, proj.reshape(blocks, rhs, rhs), factor)


def solution(mesh):
    finer = Mesh(mesh.devices.reshape(4, 2, 4, 4), ALL)
    in_specs = (
        P(None, None, ALL),
        P(ALL, None, None, None),
        P(ALL, None),
        P(ALL),
        P(ALL, None, None),
        P(),
        P(ALL, None, None),
        P(ALL, None),
        P(ALL, None),
        P(ALL, None),
    )
    out_specs = (P(None, ALL), P(), P())
    return jax.shard_map(
        shards, mesh=finer, in_specs=in_specs, out_specs=out_specs, check_vma=False
    )
```

```python
import functools

import jax
import jax.numpy as jnp
from jax import lax
from jax.experimental import pallas as pl
from jax.experimental.pallas import tpu as pltpu
from jax.sharding import Mesh
from jax.sharding import PartitionSpec as P

ALL = ("x", "c", "y", "z")
ORDERS = (("x", "y", "z"), ("y", "z", "x"), ("z", "x", "y"))
MESH = pl.DeviceIdType.MESH
F32, BF16 = jnp.float32, jnp.bfloat16
LIMIT = 67043328
NT = (((1,), (1,)), ((), ()))
TN = (((0,), (0,)), ((), ()))


def dot(a, b, dims=(((1,), (0,)), ((), ()))):
    return lax.dot_general(a, b, dims, preferred_element_type=F32)


def halves(values):
    upper = values.astype(BF16)
    return upper, (values - upper.astype(F32)).astype(BF16)


def step_kernel(
    cuts, total_rows, basis_ref, p_ref, near_blocks_ref, m2l_ref, list_ref, count_ref,
    src_ref, near_count_ref, far_ref, class_ref,
    stack_ref, proj_ref, left_ref, factor_ref,
    proj_buf, out_sem, all_ref, xbuf, nbuf, pbuf, mbuf, stage, lists, base_ref, vbuf, mats, table_ref, table,
    inner_ref, gram_in, one_in, two_in, stack, piece, whole, gone, narrow, two_gone, gram_out,
    s1, r1, s2, r2, s3, r3, v_sem, m_sem, t_sem,
    send_sem, recv_sem, sib_send, sib_recv, halo_send, halo_recv, list_send, list_recv,
    own_sem, x_sem, p_sem, stage_sem, nsem,
):
    me = {name: lax.axis_index(name) for name in ALL}
    leaves = near_blocks_ref.shape[0]
    slots = near_blocks_ref.shape[1]
    panels = near_blocks_ref.shape[2]
    depth = nbuf.shape[0]
    column = me["x"] * 2 + me["c"]

    def at(axis, by):
        return lax.rem(me[axis] + (by + 4), 4)

    def near_copy(leaf, slot):
        return pltpu.make_async_copy(near_blocks_ref.at[leaf], nbuf.at[slot], nsem.at[slot])

    blocks, rhs = basis_ref.shape[:2]
    mine = xbuf.at[pl.ds(leaves, leaves)]
    for leaf in range(leaves):
        pltpu.make_async_copy(
            basis_ref.at[blocks - 1, :, pl.ds(leaf * panels, panels)], mine.at[leaf], x_sem
        ).start()
    load_p = pltpu.make_async_copy(p_ref, pbuf, p_sem)
    load_p.start()
    load_v = pltpu.make_async_copy(basis_ref, vbuf, v_sem)
    load_v.start()
    classes, terms = m2l_ref.shape[:2]
    load_m = pltpu.make_async_copy(m2l_ref, mats.at[pl.ds(0, classes)], m_sem)
    load_m.start()
    mats[classes] = jnp.zeros((terms, terms), BF16)
    for leaf in range(depth):
        near_copy(leaf, leaf).start()

    other = {"c": 1 - me["c"]}
    barrier = pltpu.get_barrier_semaphore()
    gx = 8

    def col_peer(by):
        c = lax.rem(column + by, gx)
        return c, {"x": c // 2, "c": lax.rem(c, 2)}

    def line_peer(axis, by):
        c = lax.rem(me[axis] + by, 4)
        return c, {axis: c}

    after, before = col_peer(1)[1], col_peer(gx - 1)[1]
    peers = [col_peer(by)[1] for by in range(1, gx)]
    peers += [line_peer(axis, by)[1] for axis in ("y", "z") for by in range(1, 4)]
    for peer in peers:
        pl.semaphore_signal(barrier, inc=1, device_id=peer, device_id_type=MESH)
    slots_out = list_ref.shape[1]
    stage[...] = jnp.zeros_like(stage)
    stage[:slots_out, :] = list_ref[0]
    stage[slots_out : slots_out + 1, :] = count_ref[...]
    def list_region(stage_index):
        index = [me["x"], me["c"], me["y"], me["z"]]
        for place_of in ((), (0,), (0, 2), (0, 2, 3))[stage_index]:
            index[place_of] = slice(None)
        return lists.at[tuple(index)]

    def list_copies(i):
        if i == 3:
            targets = [other]
        else:
            axis = ("x", "y", "z")[i]
            targets = [{axis: at(axis, by)} for by in (1, 2, 3)]
        region = list_region(i)
        out = []
        for t, target in enumerate(targets):
            out.append(
                pltpu.make_async_remote_copy(
                    src_ref=region, dst_ref=region,
                    send_sem=list_send.at[i, t], recv_sem=list_recv.at[i, t],
                    device_id=target, device_id_type=MESH,
                )
            )
        return out

    list_sent = []

    def lists_go(i):
        for copy in list_copies(i):
            copy.start()
            list_sent.append(copy)

    def lists_come(i):
        for copy in list_copies(i):
            copy.wait_recv()

    my_list = lists.at[me["x"], me["c"], me["y"], me["z"]]
    keep_list = pltpu.make_async_copy(stage, my_list, stage_sem)
    keep_list.start()
    pltpu.make_async_copy(mine, mine, x_sem).wait()
    load_p.wait()
    keep_list.wait()
    pl.semaphore_wait(barrier, len(peers))
    lists_go(0)

    def multipole(leaf, carry):
        block = dot(xbuf[leaves + leaf], pbuf[leaf]).astype(BF16)
        mbuf[2 * leaf] = block[: rhs // 2]
        mbuf[2 * leaf + 1] = block[rhs // 2 :]
        return carry

    lax.fori_loop(0, leaves, multipole, 0, unroll=4)
    here = all_ref.at[me["x"], me["c"], me["y"], me["z"]]
    keep = pltpu.make_async_copy(mbuf, here, own_sem)
    keep.start()

    def place(where, rows, core):
        index = []
        for name in ALL:
            if name == "c":
                index.append(core)
            elif name in where:
                index.append(where[name])
            else:
                index.append(slice(None))
        return all_ref.at[tuple(index) + (pl.ds(rows[0], rows[1] - rows[0]),)]

    units = [(0, None, None)]
    units += [(1, r, None) for r in (0, -1, 1, 2)]
    units += [(2, r, 0) for r in (0, -1, 1, 2)]
    units += [(2, None, r) for r in (-1, 1, 2)]
    number = {u: i for i, u in enumerate(units)}
    started = []

    def where_of(colour, unit, by):
        axes = ORDERS[colour]
        phase, first, second = unit
        where = {}
        if phase == 0:
            where = {axes[0]: by, axes[1]: 0, axes[2]: 0}
        elif phase == 1:
            where = {axes[0]: first, axes[1]: by, axes[2]: 0}
        else:
            where = {axes[1]: second, axes[2]: by}
            if first is not None:
                where[axes[0]] = first
        return where

    def rows_of(colour, part):
        low, high = cuts[colour], cuts[colour + 1]
        middle = low + (high - low) // 2
        return {"all": (low, high), "lower": (low, middle), "upper": (middle, high)}[part]

    def remote(colour, unit, kind):
        axis = ORDERS[colour][unit[0]]
        by, to, part = ((0, 1, "all"), (0, -1, "all"), (-1, 1, "lower"), (1, -1, "upper"))[kind]
        offsets = where_of(colour, unit, by)
        where = {name: at(name, v) for name, v in offsets.items()}
        rows = rows_of(colour, part)
        dst = place(where, rows, me["c"])
        i = number[unit]
        return pltpu.make_async_remote_copy(
            src_ref=dst,
            dst_ref=dst,
            send_sem=send_sem.at[colour, i, kind],
            recv_sem=recv_sem.at[colour, i, kind],
            device_id={axis: at(axis, to)},
            device_id_type=MESH,
        )

    def send(colour, unit):
        for kind in (0, 1):
            copy = remote(colour, unit, kind)
            copy.start()
            started.append(copy)

    def arrived(colour, unit):
        for kind in (0, 1):
            remote(colour, unit, kind).wait_recv()
        for kind in (2, 3):
            copy = remote(colour, unit, kind)
            copy.start()
            started.append(copy)

    def arrived_far(colour, unit):
        for kind in (2, 3):
            remote(colour, unit, kind).wait_recv()

    crossings = []

    def cross(colour, second, third):
        axes = ORDERS[colour]
        where = {axes[1]: at(axes[1], second), axes[2]: at(axes[2], third)}
        ref = place(where, rows_of(colour, "all"), me["c"])
        i = ((0, -1, 1, 2).index(second)) * 4 + (0, -1, 1, 2).index(third)
        copy = pltpu.make_async_remote_copy(
            src_ref=ref,
            dst_ref=ref,
            send_sem=sib_send.at[colour, i],
            recv_sem=sib_recv.at[colour, i],
            device_id=other,
            device_id_type=MESH,
        )
        copy.start()
        other_ref = place(where, rows_of(colour, "all"), other["c"])
        arrival = pltpu.make_async_remote_copy(
            src_ref=other_ref,
            dst_ref=other_ref,
            send_sem=sib_send.at[colour, i],
            recv_sem=sib_recv.at[colour, i],
            device_id=other,
            device_id_type=MESH,
        )
        crossings.append((copy, arrival))

    done_leaves = [0]

    def near(count):
        first = done_leaves[0]
        last = min(leaves, first + count)
        done_leaves[0] = last
        if last == first:
            return
        if first == 0:
            for copy in halo:
                copy.wait_recv()

            @pl.when(column == 0)
            def _():
                xbuf[:leaves] = jnp.zeros((leaves,) + xbuf.shape[1:], BF16)

            @pl.when(column == gx - 1)
            def _():
                xbuf[2 * leaves :] = jnp.zeros((leaves,) + xbuf.shape[1:], BF16)

        def body(leaf, carry):
            slot = lax.rem(leaf, depth)
            near_copy(leaf, slot).wait()
            lanes = pl.ds(pl.multiple_of(leaf * panels, panels), panels)
            total = xbuf[leaves + leaf].astype(F32)
            for k in range(slots):
                live = lax.min(lax.max(near_count_ref[leaf] - k, 0), 1).astype(F32)
                total = total + live * dot(xbuf[src_ref[k, leaf]], nbuf[slot, k], NT)
            base_ref[:, lanes] = total

            @pl.when(leaf + depth < leaves)
            def _():
                near_copy(leaf + depth, slot).start()

            return carry

        lax.fori_loop(first, last, body, 0)

    colours = range(3)
    keep.wait()
    for k in colours:
        send(k, units[0])
    lists_come(0)
    lists_go(1)
    for k in colours:
        send(k, (1, 0, None))
    for k in colours:
        arrived(k, units[0])
        for r in (-1, 1):
            send(k, (1, r, None))
    lists_come(1)
    lists_go(2)
    for k in colours:
        arrived_far(k, units[0])
        send(k, (1, 2, None))
    for k in colours:
        send(k, (2, 0, 0))
    for k in colours:
        arrived(k, (1, 0, None))
        for r in (-1, 1, 2):
            send(k, (2, r, 0))
    for k in colours:
        cross(k, 0, 0)
    for r in (-1, 1, 2):
        for k in colours:
            arrived(k, (1, r, None))
    for k in colours:
        arrived(k, (2, 0, 0))
    for r in (-1, 1):
        for k in colours:
            send(k, (2, None, r))
    halo = []
    for i, (target, slot) in enumerate(((after, 0), (before, 2))):
        copy = pltpu.make_async_remote_copy(
            src_ref=mine,
            dst_ref=xbuf.at[pl.ds(slot * leaves, leaves)],
            send_sem=halo_send.at[i],
            recv_sem=halo_recv.at[i],
            device_id=target,
            device_id_type=MESH,
        )
        copy.start()
        halo.append(copy)
    for r in (0, -1, 1, 2):
        for k in colours:
            arrived_far(k, (1, r, None))
    for k in colours:
        send(k, (2, None, 2))
    for r in (-1, 1, 2):
        for k in colours:
            cross(k, r, 0)
    lists_come(2)
    lists_go(3)
    for r in (-1, 1, 2):
        for k in colours:
            arrived(k, (2, r, 0))
    for k in colours:
        for t in (-1, 1):
            cross(k, 0, t)
    for r in (-1, 1):
        for k in colours:
            arrived(k, (2, None, r))
            for t in (-1, 1):
                cross(k, r, t)
            if r == 1:
                near(2)
    for r in (0, -1, 1, 2):
        for k in colours:
            arrived_far(k, (2, r, 0))
        near(2)
    for k in colours:
        cross(k, 0, 2)
    near(leaves)
    lists_come(3)
    index = ((me["x"] * 2 + me["c"]) * 4 + me["y"]) * 4 + me["z"]
    peers_all = lists.shape[-1]
    mark = (lax.broadcasted_iota(jnp.int32, (8, peers_all), 1) == index).astype(BF16)
    picked = dot(mark, lists[...].reshape(-1, peers_all).astype(F32).astype(BF16), NT)
    table_ref[...] = picked[:1].astype(jnp.int32)
    to_scalar = pltpu.make_async_copy(table_ref, table, t_sem)
    to_scalar.start()
    for k in colours:
        arrived(k, (2, None, 2))
        for t in (-1, 1):
            cross(k, 2, t)
    for r in (-1, 1, 2):
        for k in colours:
            arrived_far(k, (2, None, r))
            cross(k, r, 2)
    for copy, arrival in crossings:
        arrival.wait_recv()
    to_scalar.wait()
    load_m.wait()
    load_v.wait()
    far_slots = far_ref.shape[1]
    inner_ref[...] = jnp.zeros_like(inner_ref)

    group = 4

    def expansion(leaf):
        total = jnp.zeros((rhs, terms), F32)
        for pair in range(far_slots // 2):
            sources, steps = [], []
            for e in (2 * pair, 2 * pair + 1):
                f = far_ref[leaf, e]
                sender = lax.shift_right_logical(f, 2)
                slot = f & 3
                unit = lax.min(lax.max(table[0, sender * 8 + slot], 0), leaves - 1) * 2
                live = lax.min(lax.max(table[0, sender * 8 + 4] - slot, 0), 1)
                which = classes - live * (classes - class_ref[leaf, e])
                place_x = lax.shift_right_logical(sender, 5)
                place_c = lax.shift_right_logical(sender, 4) & 1
                place_y = lax.shift_right_logical(sender, 2) & 3
                place_z = sender & 3
                sources.append(
                    jnp.concatenate(
                        [
                            all_ref[place_x, place_c, place_y, place_z, unit],
                            all_ref[place_x, place_c, place_y, place_z, unit + 1],
                        ],
                        axis=0,
                    )
                )
                steps.append(mats[which])
            total = total + dot(
                jnp.concatenate(sources, axis=1), jnp.concatenate(steps, axis=0)
            )
        return total.astype(BF16)

    def far(g, carry):
        first = g * group
        local = [expansion(first + j) for j in range(group)]
        for j in range(group):
            lanes = pl.ds(pl.multiple_of((first + j) * panels, panels), panels)
            base_ref[:, lanes] += dot(local[j], pbuf[first + j], NT)
        width = group * panels
        lanes = pl.ds(pl.multiple_of(g * width, width), width)
        both = jnp.concatenate(halves(base_ref[:, lanes]), axis=0)
        out = dot(both, vbuf[:, :, lanes].reshape(blocks * rhs, width), NT)
        inner_ref[...] += out[:rhs] + out[rhs:]
        return carry

    lax.fori_loop(0, leaves // group, far, 0)
    columns = leaves * panels
    def send_to(src, dst, send, recv, peer):
        return pltpu.make_async_remote_copy(
            src_ref=src, dst_ref=dst, send_sem=send, recv_sem=recv,
            device_id=peer, device_id_type=MESH,
        )

    def all_reduce(n, source, arrivals, mine, parts, result):
        rows = rhs // gx
        sent = []
        for by in range(1, gx):
            c, peer = col_peer(by)
            at = pl.ds(pl.multiple_of(c * rows, rows), rows)
            copy = send_to(source.at[at], arrivals.at[gx - by], s1.at[n, by], r1.at[n, gx - by], peer)
            copy.start()
            sent.append(copy)
        own = pl.ds(pl.multiple_of(column * rows, rows), rows)
        total = source[own, :]
        for by in range(1, gx):
            send_to(arrivals.at[by], arrivals.at[by], s1.at[n, by], r1.at[n, by], col_peer(1)[1]).wait_recv()
            total = total + arrivals[by]
        for n_axis, axis in enumerate(("y", "z")):
            slot = mine.at[n_axis]
            slot[...] = total
            for by in range(1, 4):
                i = n_axis * 4 + by
                copy = send_to(
                    slot, parts.at[n_axis * 4 + me[axis]],
                    s2.at[n, i], r2.at[n, n_axis * 4 + 4 - by], line_peer(axis, by)[1],
                )
                copy.start()
                sent.append(copy)
            parts[n_axis * 4 + me[axis]] = total
            for by in range(1, 4):
                c, peer = line_peer(axis, by)
                i = n_axis * 4 + by
                send_to(slot, parts.at[n_axis * 4 + c], s2.at[n, i], r2.at[n, i], peer).wait_recv()
            total = parts[n_axis * 4]
            for c in range(1, 4):
                total = total + parts[n_axis * 4 + c]
        result[own, :] = total
        for by in range(1, gx):
            c, peer = col_peer(by)
            copy = send_to(result.at[own], result.at[own], s3.at[n, by], r3.at[n, gx - by], peer)
            copy.start()
            sent.append(copy)
        for by in range(1, gx):
            c, peer = col_peer(by)
            at = pl.ds(pl.multiple_of(c * rows, rows), rows)
            send_to(result.at[at], result.at[at], s3.at[n, by], r3.at[n, by], peer).wait_recv()
        for copy in sent:
            copy.wait_send()

    scale = 1.0 / total_rows
    all_reduce(0, inner_ref, one_in, piece, two_in, whole)
    proj = whole[...] * scale
    coef = jnp.concatenate(halves(proj), axis=0)
    step = 512
    gram = jnp.zeros((2 * rhs, 2 * rhs), F32)
    for i in range(0, columns, step):
        v = vbuf[:, :, i : i + step].reshape(blocks * rhs, step)
        out = dot(coef, v)
        resid = base_ref[:, i : i + step] - (out[:rhs] + out[rhs:])
        both = jnp.concatenate(halves(resid), axis=0)
        stack[:, i : i + step] = both
        gram = gram + dot(both, both, NT)
    gram_in[...] = gram[:rhs] + gram[rhs:]
    for i in range(0, blocks * rhs, 2 * rhs):
        proj_buf[i : i + 2 * rhs, :] = proj[:, i : i + 2 * rhs].T
    leaving = [
        pltpu.make_async_copy(stack, stack_ref, out_sem.at[0]),
        pltpu.make_async_copy(proj_buf, proj_ref, out_sem.at[1]),
    ]
    for copy in leaving:
        copy.start()
    all_reduce(1, gram_in, gone, narrow, two_gone, gram_out)
    folded = gram_out[...] * scale
    folded = folded + pltpu.roll(folded, rhs, 1)
    lane = lax.broadcasted_iota(jnp.int32, (rhs, 2 * rhs), 1)
    row = lax.broadcasted_iota(jnp.int32, (rhs, 2 * rhs), 0)
    work = jnp.where(lane < rhs, folded, (lane - rhs == row).astype(F32))
    tall = 8
    count = rhs // tall
    part = [work[i * tall : (i + 1) * tall] for i in range(count)]
    low = lax.broadcasted_iota(jnp.int32, (tall, 2 * rhs), 0)
    for b in range(count):
        cols = [
            {i: jnp.broadcast_to(part[i][:, b * tall + t : b * tall + t + 1], (tall, 2 * rhs)) for i in range(b, count)}
            for t in range(tall)
        ]
        for t in range(tall):
            inverse = 1.0 / cols[t][b][t : t + 1, :]
            across = {u: cols[u][b][t : t + 1, :] * inverse for u in range(t + 1, tall)}
            pivot = part[b][t : t + 1, :] * inverse
            for i in range(b, count):
                factor = cols[t][i]
                if i == b:
                    factor = jnp.where(low > t, factor, 0.0)
                part[i] = part[i] - factor * pivot
                for u in range(t + 1, tall):
                    cols[u][i] = cols[u][i] - factor * across[u]
    work = jnp.concatenate(part, axis=0)
    diagonal = jnp.sum(jnp.where(lane == row, work, 0.0), axis=1, keepdims=True)
    work = work * lax.rsqrt(diagonal)
    factor_ref[...] = jnp.where((lane >= row) & (lane < rhs), work, 0.0).T[:rhs]
    right = jnp.where(lane < rhs, 0.0, work)
    right = right + pltpu.roll(right, rhs, 1)
    left_ref[...] = jnp.concatenate(halves(right), axis=0)
    for copy in leaving:
        copy.wait()
    for copy, arrival in crossings:
        copy.wait_send()
    for copy in started + list_sent:
        copy.wait_send()
    for copy in halo:
        copy.wait_send()


def step(basis, p2m, near_blocks, m2l, send_list, send_count, near_src, near_count, far_src, far_class):
    leaves, slots, panels, _ = near_blocks.shape
    blocks, rhs, columns = basis.shape
    classes, terms = m2l.shape[:2]
    peers = send_list.shape[1]
    units = 2 * leaves
    wide = blocks * rhs
    cuts = (0, 11, 21, units)
    depth = 4
    hbm = pl.BlockSpec(memory_space=pltpu.HBM)
    vmem = pl.BlockSpec(memory_space=pltpu.VMEM)
    smem = pl.BlockSpec(memory_space=pltpu.SMEM)
    dma = pltpu.SemaphoreType.DMA
    return pl.pallas_call(
        functools.partial(step_kernel, cuts, columns * peers),
        in_specs=[hbm, hbm, hbm, hbm, vmem, vmem, smem, smem, smem, smem],
        out_specs=(hbm, hbm, vmem, vmem),
        out_shape=(
            jax.ShapeDtypeStruct((2 * rhs, columns), BF16),
            jax.ShapeDtypeStruct((wide, rhs), F32),
            jax.ShapeDtypeStruct((2 * rhs, 2 * rhs), BF16),
            jax.ShapeDtypeStruct((rhs, rhs), F32),
        ),
        scratch_shapes=[
            pltpu.VMEM((wide, rhs), F32),
            dma((2,)),
            pltpu.VMEM((4, 2, 4, 4, units, rhs // 2, terms), BF16),
            pltpu.VMEM((3 * leaves, rhs, panels), BF16),
            pltpu.VMEM((depth, slots, panels, panels), BF16),
            pltpu.VMEM((leaves, panels, terms), BF16),
            pltpu.VMEM((units, rhs // 2, terms), BF16),
            pltpu.VMEM((8, peers), jnp.int32),
            pltpu.VMEM((4, 2, 4, 4, 8, peers), jnp.int32),
            pltpu.VMEM((rhs, columns), F32),
            pltpu.VMEM((blocks, rhs, columns), BF16),
            pltpu.VMEM((classes + 1, terms, terms), BF16),
            pltpu.VMEM((1, peers * 8), jnp.int32),
            pltpu.SMEM((1, peers * 8), jnp.int32),
            pltpu.VMEM((rhs, wide), F32),
            pltpu.VMEM((rhs, 2 * rhs), F32),
            pltpu.VMEM((8, 8, wide), F32),
            pltpu.VMEM((8, 8, wide), F32),
            pltpu.VMEM((2 * rhs, columns), BF16),
            pltpu.VMEM((2, 8, wide), F32),
            pltpu.VMEM((rhs, wide), F32),
            pltpu.VMEM((8, 8, 2 * rhs), F32),
            pltpu.VMEM((2, 8, 2 * rhs), F32),
            pltpu.VMEM((8, 8, 2 * rhs), F32),
            pltpu.VMEM((rhs, 2 * rhs), F32),
            dma((2, 8)), dma((2, 8)), dma((2, 8)), dma((2, 8)), dma((2, 8)), dma((2, 8)),
            dma, dma, dma,
            dma((3, 12, 4)), dma((3, 12, 4)), dma((3, 16)), dma((3, 16)),
            dma((2,)), dma((2,)), dma((4, 3)), dma((4, 3)),
            dma, dma, dma, dma, dma((depth,)),
        ],
        compiler_params=pltpu.CompilerParams(
            collective_id=0, has_side_effects=True, vmem_limit_bytes=LIMIT
        ),
        name="step",
    )(
        basis, p2m, near_blocks, m2l, jnp.swapaxes(send_list, 1, 2), send_count,
        near_src.T, near_count, far_src, far_class,
    )


def last_kernel(stack_ref, proj_in, left_ref, factor_in, next_ref, proj_ref, factor_ref):
    rhs = next_ref.shape[0]

    @pl.when(pl.program_id(0) == 0)
    def _():
        proj_ref[...] = proj_in[...]
        factor_ref[...] = factor_in[...]

    out = dot(left_ref[...], stack_ref[...])
    next_ref[...] = (out[:rhs] + out[rhs:]).astype(BF16)


def last(stack, proj, left, factor):
    double, columns = stack.shape
    rhs = double // 2
    steps = 4

    def fixed(array):
        return pl.BlockSpec(array.shape, lambda i: (0, 0))

    return pl.pallas_call(
        last_kernel,
        grid=(steps,),
        in_specs=[
            pl.BlockSpec((double, columns // steps), lambda i: (0, i)),
            fixed(proj), fixed(left), fixed(factor),
        ],
        out_specs=(
            pl.BlockSpec((rhs, columns // steps), lambda i: (0, i)), fixed(proj), fixed(factor),
        ),
        out_shape=(
            jax.ShapeDtypeStruct((rhs, columns), BF16),
            jax.ShapeDtypeStruct(proj.shape, F32),
            jax.ShapeDtypeStruct(factor.shape, F32),
        ),
        compiler_params=pltpu.CompilerParams(vmem_limit_bytes=LIMIT),
        name="last",
    )(stack, proj, left, factor)


def shards(
    basis, near_blocks, near_src, near_count, p2m, m2l, send_list, send_count, far_src, far_class
):
    blocks, rhs, columns = basis.shape
    stack, proj, left, factor = step(
        basis, p2m, near_blocks, m2l, send_list, send_count, near_src, near_count, far_src, far_class
    )
    new, proj, factor = last(stack, proj, left, factor)
    return (new, proj.reshape(blocks, rhs, rhs), factor)


def solution(mesh):
    finer = Mesh(mesh.devices.reshape(4, 2, 4, 4), ALL)
    in_specs = (
        P(None, None, ALL),
        P(ALL, None, None, None),
        P(ALL, None),
        P(ALL),
        P(ALL, None, None),
        P(),
        P(ALL, None, None),
        P(ALL, None),
        P(ALL, None),
        P(ALL, None),
    )
    out_specs = (P(None, ALL), P(), P())
    return jax.shard_map(
        shards, mesh=finer, in_specs=in_specs, out_specs=out_specs, check_vma=False
    )
```

```python
import functools

import jax
import jax.numpy as jnp
from jax import lax
from jax.experimental import pallas as pl
from jax.experimental.pallas import tpu as pltpu
from jax.sharding import Mesh
from jax.sharding import PartitionSpec as P

ALL = ("x", "c", "y", "z")
ORDERS = (("x", "y", "z"), ("y", "z", "x"), ("z", "x", "y"))
MESH = pl.DeviceIdType.MESH
F32, BF16 = jnp.float32, jnp.bfloat16
LIMIT = 67043328
NT = (((1,), (1,)), ((), ()))
TN = (((0,), (0,)), ((), ()))


def dot(a, b, dims=(((1,), (0,)), ((), ()))):
    return lax.dot_general(a, b, dims, preferred_element_type=F32)


def halves(values):
    upper = values.astype(BF16)
    return upper, (values - upper.astype(F32)).astype(BF16)


def step_kernel(
    cuts, total_rows, basis_ref, p_ref, near_blocks_ref, m2l_ref, list_ref, count_ref,
    src_ref, near_count_ref, far_ref, class_ref,
    stack_ref, proj_ref, left_ref, factor_ref,
    proj_buf, out_sem, all_ref, xbuf, nbuf, pbuf, mbuf, stage, lists, base_ref, vbuf, mats, table_ref, table,
    inner_ref, gram_in, one_in, two_in, stack, piece, whole, gone, narrow, two_gone, gram_out,
    s1, r1, s2, r2, s3, r3, v_sem, m_sem, t_sem,
    send_sem, recv_sem, sib_send, sib_recv, halo_send, halo_recv, list_send, list_recv,
    own_sem, x_sem, p_sem, stage_sem, nsem,
):
    me = {name: lax.axis_index(name) for name in ALL}
    leaves = near_blocks_ref.shape[0]
    slots = near_blocks_ref.shape[1]
    panels = near_blocks_ref.shape[2]
    depth = nbuf.shape[0]
    column = me["x"] * 2 + me["c"]

    def at(axis, by):
        return lax.rem(me[axis] + (by + 4), 4)

    def near_copy(leaf, slot):
        return pltpu.make_async_copy(near_blocks_ref.at[leaf], nbuf.at[slot], nsem.at[slot])

    blocks, rhs = basis_ref.shape[:2]
    mine = xbuf.at[pl.ds(leaves, leaves)]
    for leaf in range(leaves):
        pltpu.make_async_copy(
            basis_ref.at[blocks - 1, :, pl.ds(leaf * panels, panels)], mine.at[leaf], x_sem
        ).start()
    load_p = pltpu.make_async_copy(p_ref, pbuf, p_sem)
    load_p.start()
    load_v = pltpu.make_async_copy(basis_ref, vbuf, v_sem)
    load_v.start()
    classes, terms = m2l_ref.shape[:2]
    load_m = pltpu.make_async_copy(m2l_ref, mats.at[pl.ds(0, classes)], m_sem)
    load_m.start()
    mats[classes] = jnp.zeros((terms, terms), BF16)
    for leaf in range(depth):
        near_copy(leaf, leaf).start()

    other = {"c": 1 - me["c"]}
    barrier = pltpu.get_barrier_semaphore()
    gx = 8

    def col_peer(by):
        c = lax.rem(column + by, gx)
        return c, {"x": c // 2, "c": lax.rem(c, 2)}

    def line_peer(axis, by):
        c = lax.rem(me[axis] + by, 4)
        return c, {axis: c}

    after, before = col_peer(1)[1], col_peer(gx - 1)[1]
    peers = [col_peer(by)[1] for by in range(1, gx)]
    peers += [line_peer(axis, by)[1] for axis in ("y", "z") for by in range(1, 4)]
    for peer in peers:
        pl.semaphore_signal(barrier, inc=1, device_id=peer, device_id_type=MESH)
    slots_out = list_ref.shape[1]
    stage[...] = jnp.zeros_like(stage)
    stage[:slots_out, :] = list_ref[0]
    stage[slots_out : slots_out + 1, :] = count_ref[...]
    def list_region(stage_index):
        index = [me["x"], me["c"], me["y"], me["z"]]
        for place_of in ((), (0,), (0, 2), (0, 2, 3))[stage_index]:
            index[place_of] = slice(None)
        return lists.at[tuple(index)]

    def list_copies(i):
        if i == 3:
            targets = [other]
        else:
            axis = ("x", "y", "z")[i]
            targets = [{axis: at(axis, by)} for by in (1, 2, 3)]
        region = list_region(i)
        out = []
        for t, target in enumerate(targets):
            out.append(
                pltpu.make_async_remote_copy(
                    src_ref=region, dst_ref=region,
                    send_sem=list_send.at[i, t], recv_sem=list_recv.at[i, t],
                    device_id=target, device_id_type=MESH,
                )
            )
        return out

    list_sent = []

    def lists_go(i):
        for copy in list_copies(i):
            copy.start()
            list_sent.append(copy)

    def lists_come(i):
        for copy in list_copies(i):
            copy.wait_recv()

    my_list = lists.at[me["x"], me["c"], me["y"], me["z"]]
    keep_list = pltpu.make_async_copy(stage, my_list, stage_sem)
    keep_list.start()
    pltpu.make_async_copy(mine, mine, x_sem).wait()
    load_p.wait()
    keep_list.wait()
    pl.semaphore_wait(barrier, len(peers))
    lists_go(0)

    def multipole(leaf, carry):
        block = dot(xbuf[leaves + leaf], pbuf[leaf]).astype(BF16)
        mbuf[2 * leaf] = block[: rhs // 2]
        mbuf[2 * leaf + 1] = block[rhs // 2 :]
        return carry

    lax.fori_loop(0, leaves, multipole, 0, unroll=4)
    here = all_ref.at[me["x"], me["c"], me["y"], me["z"]]
    keep = pltpu.make_async_copy(mbuf, here, own_sem)
    keep.start()

    def place(where, rows, core):
        index = []
        for name in ALL:
            if name == "c":
                index.append(core)
            elif name in where:
                index.append(where[name])
            else:
                index.append(slice(None))
        return all_ref.at[tuple(index) + (pl.ds(rows[0], rows[1] - rows[0]),)]

    units = [(0, None, None)]
    units += [(1, r, None) for r in (0, -1, 1, 2)]
    units += [(2, r, 0) for r in (0, -1, 1, 2)]
    units += [(2, None, r) for r in (-1, 1, 2)]
    number = {u: i for i, u in enumerate(units)}
    started = []

    def where_of(colour, unit, by):
        axes = ORDERS[colour]
        phase, first, second = unit
        where = {}
        if phase == 0:
            where = {axes[0]: by, axes[1]: 0, axes[2]: 0}
        elif phase == 1:
            where = {axes[0]: first, axes[1]: by, axes[2]: 0}
        else:
            where = {axes[1]: second, axes[2]: by}
            if first is not None:
                where[axes[0]] = first
        return where

    def rows_of(colour, part):
        low, high = cuts[colour], cuts[colour + 1]
        middle = low + (high - low) // 2
        return {"all": (low, high), "lower": (low, middle), "upper": (middle, high)}[part]

    def remote(colour, unit, kind):
        axis = ORDERS[colour][unit[0]]
        by, to, part = ((0, 1, "all"), (0, -1, "all"), (-1, 1, "lower"), (1, -1, "upper"))[kind]
        offsets = where_of(colour, unit, by)
        where = {name: at(name, v) for name, v in offsets.items()}
        rows = rows_of(colour, part)
        dst = place(where, rows, me["c"])
        i = number[unit]
        return pltpu.make_async_remote_copy(
            src_ref=dst,
            dst_ref=dst,
            send_sem=send_sem.at[colour, i, kind],
            recv_sem=recv_sem.at[colour, i, kind],
            device_id={axis: at(axis, to)},
            device_id_type=MESH,
        )

    def send(colour, unit):
        for kind in (0, 1):
            copy = remote(colour, unit, kind)
            copy.start()
            started.append(copy)

    def arrived(colour, unit):
        for kind in (0, 1):
            remote(colour, unit, kind).wait_recv()
        for kind in (2, 3):
            copy = remote(colour, unit, kind)
            copy.start()
            started.append(copy)

    def arrived_far(colour, unit):
        for kind in (2, 3):
            remote(colour, unit, kind).wait_recv()

    crossings = []

    def cross(colour, second, third):
        axes = ORDERS[colour]
        where = {axes[1]: at(axes[1], second), axes[2]: at(axes[2], third)}
        ref = place(where, rows_of(colour, "all"), me["c"])
        i = ((0, -1, 1, 2).index(second)) * 4 + (0, -1, 1, 2).index(third)
        copy = pltpu.make_async_remote_copy(
            src_ref=ref,
            dst_ref=ref,
            send_sem=sib_send.at[colour, i],
            recv_sem=sib_recv.at[colour, i],
            device_id=other,
            device_id_type=MESH,
        )
        copy.start()
        other_ref = place(where, rows_of(colour, "all"), other["c"])
        arrival = pltpu.make_async_remote_copy(
            src_ref=other_ref,
            dst_ref=other_ref,
            send_sem=sib_send.at[colour, i],
            recv_sem=sib_recv.at[colour, i],
            device_id=other,
            device_id_type=MESH,
        )
        crossings.append((copy, arrival))

    done_leaves = [0]

    def near(count):
        first = done_leaves[0]
        last = min(leaves, first + count)
        done_leaves[0] = last
        if last == first:
            return
        if first == 0:
            for copy in halo:
                copy.wait_recv()

            @pl.when(column == 0)
            def _():
                xbuf[:leaves] = jnp.zeros((leaves,) + xbuf.shape[1:], BF16)

            @pl.when(column == gx - 1)
            def _():
                xbuf[2 * leaves :] = jnp.zeros((leaves,) + xbuf.shape[1:], BF16)

        def body(leaf, carry):
            slot = lax.rem(leaf, depth)
            near_copy(leaf, slot).wait()
            lanes = pl.ds(pl.multiple_of(leaf * panels, panels), panels)
            total = xbuf[leaves + leaf].astype(F32)
            for k in range(slots):
                live = lax.min(lax.max(near_count_ref[leaf] - k, 0), 1).astype(F32)
                total = total + live * dot(xbuf[src_ref[k, leaf]], nbuf[slot, k], NT)
            base_ref[:, lanes] = total

            @pl.when(leaf + depth < leaves)
            def _():
                near_copy(leaf + depth, slot).start()

            return carry

        lax.fori_loop(first, last, body, 0)

    colours = range(3)
    keep.wait()
    for k in colours:
        send(k, units[0])
    lists_come(0)
    lists_go(1)
    for k in colours:
        send(k, (1, 0, None))
    for k in colours:
        arrived(k, units[0])
        for r in (-1, 1):
            send(k, (1, r, None))
    lists_come(1)
    lists_go(2)
    for k in colours:
        arrived_far(k, units[0])
        send(k, (1, 2, None))
    for k in colours:
        send(k, (2, 0, 0))
    for k in colours:
        arrived(k, (1, 0, None))
        for r in (-1, 1, 2):
            send(k, (2, r, 0))
    for k in colours:
        cross(k, 0, 0)
    for r in (-1, 1, 2):
        for k in colours:
            arrived(k, (1, r, None))
    for k in colours:
        arrived(k, (2, 0, 0))
    for r in (-1, 1):
        for k in colours:
            send(k, (2, None, r))
    halo = []
    for i, (target, slot) in enumerate(((after, 0), (before, 2))):
        copy = pltpu.make_async_remote_copy(
            src_ref=mine,
            dst_ref=xbuf.at[pl.ds(slot * leaves, leaves)],
            send_sem=halo_send.at[i],
            recv_sem=halo_recv.at[i],
            device_id=target,
            device_id_type=MESH,
        )
        copy.start()
        halo.append(copy)
    for r in (0, -1, 1, 2):
        for k in colours:
            arrived_far(k, (1, r, None))
    for k in colours:
        send(k, (2, None, 2))
    for r in (-1, 1, 2):
        for k in colours:
            cross(k, r, 0)
    lists_come(2)
    lists_go(3)
    for r in (-1, 1, 2):
        for k in colours:
            arrived(k, (2, r, 0))
    for k in colours:
        for t in (-1, 1):
            cross(k, 0, t)
    for r in (-1, 1):
        for k in colours:
            arrived(k, (2, None, r))
            for t in (-1, 1):
                cross(k, r, t)
            if r == 1:
                near(2)
    for r in (0, -1, 1, 2):
        for k in colours:
            arrived_far(k, (2, r, 0))
        near(2)
    for k in colours:
        cross(k, 0, 2)
    near(leaves)
    lists_come(3)
    index = ((me["x"] * 2 + me["c"]) * 4 + me["y"]) * 4 + me["z"]
    peers_all = lists.shape[-1]
    mark = (lax.broadcasted_iota(jnp.int32, (8, peers_all), 1) == index).astype(BF16)
    picked = dot(mark, lists[...].reshape(-1, peers_all).astype(F32).astype(BF16), NT)
    table_ref[...] = picked[:1].astype(jnp.int32)
    to_scalar = pltpu.make_async_copy(table_ref, table, t_sem)
    to_scalar.start()
    for k in colours:
        arrived(k, (2, None, 2))
        for t in (-1, 1):
            cross(k, 2, t)
    for r in (-1, 1, 2):
        for k in colours:
            arrived_far(k, (2, None, r))
            cross(k, r, 2)
    for copy, arrival in crossings:
        arrival.wait_recv()
    to_scalar.wait()
    load_m.wait()
    load_v.wait()
    far_slots = far_ref.shape[1]
    inner_ref[...] = jnp.zeros_like(inner_ref)

    group = 8

    flat_ref = all_ref.reshape(-1, rhs // 2, terms)

    def expansion(leaf):
        total = jnp.zeros((rhs, terms), F32)
        for pair in range(far_slots // 2):
            sources, steps = [], []
            for e in (2 * pair, 2 * pair + 1):
                f = far_ref[leaf, e]
                sender = lax.shift_right_logical(f, 2)
                slot = f & 3
                unit = lax.min(lax.max(table[0, sender * 8 + slot], 0), leaves - 1) * 2
                live = lax.min(lax.max(table[0, sender * 8 + 4] - slot, 0), 1)
                which = classes - live * (classes - class_ref[leaf, e])
                spot = sender * (2 * leaves) + unit
                sources.append(
                    jnp.concatenate(
                        [
                            flat_ref[spot],
                            flat_ref[spot + 1],
                        ],
                        axis=0,
                    )
                )
                steps.append(mats[which])
            total = total + dot(
                jnp.concatenate(sources, axis=1), jnp.concatenate(steps, axis=0)
            )
        return total.astype(BF16)

    def far(g, carry):
        first = g * group
        local = [expansion(first + j) for j in range(group)]
        for j in range(group):
            lanes = pl.ds(pl.multiple_of((first + j) * panels, panels), panels)
            base_ref[:, lanes] += dot(local[j], pbuf[first + j], NT)
        width = group * panels
        lanes = pl.ds(pl.multiple_of(g * width, width), width)
        both = jnp.concatenate(halves(base_ref[:, lanes]), axis=0)
        out = dot(both, vbuf[:, :, lanes].reshape(blocks * rhs, width), NT)
        inner_ref[...] += out[:rhs] + out[rhs:]
        return carry

    lax.fori_loop(0, leaves // group, far, 0)
    columns = leaves * panels
    def send_to(src, dst, send, recv, peer):
        return pltpu.make_async_remote_copy(
            src_ref=src, dst_ref=dst, send_sem=send, recv_sem=recv,
            device_id=peer, device_id_type=MESH,
        )

    def all_reduce(n, source, arrivals, mine, parts, result, meanwhile=None):
        rows = rhs // gx
        far_first = (4, 5, 3, 6, 2, 7, 1)
        sent = []
        for by in far_first:
            c, peer = col_peer(by)
            at = pl.ds(pl.multiple_of(c * rows, rows), rows)
            copy = send_to(source.at[at], arrivals.at[gx - by], s1.at[n, by], r1.at[n, gx - by], peer)
            copy.start()
            sent.append(copy)
        own = pl.ds(pl.multiple_of(column * rows, rows), rows)
        total = source[own, :]
        if meanwhile is not None:
            meanwhile()
        for by in range(1, gx):
            send_to(arrivals.at[by], arrivals.at[by], s1.at[n, by], r1.at[n, by], col_peer(1)[1]).wait_recv()
            total = total + arrivals[by]
        for n_axis, axis in enumerate(("y", "z")):
            slot = mine.at[n_axis]
            slot[...] = total
            for by in (2, 1, 3):
                i = n_axis * 4 + by
                copy = send_to(
                    slot, parts.at[n_axis * 4 + me[axis]],
                    s2.at[n, i], r2.at[n, n_axis * 4 + 4 - by], line_peer(axis, by)[1],
                )
                copy.start()
                sent.append(copy)
            parts[n_axis * 4 + me[axis]] = total
            for by in range(1, 4):
                c, peer = line_peer(axis, by)
                i = n_axis * 4 + by
                send_to(slot, parts.at[n_axis * 4 + c], s2.at[n, i], r2.at[n, i], peer).wait_recv()
            total = parts[n_axis * 4]
            for c in range(1, 4):
                total = total + parts[n_axis * 4 + c]
        result[own, :] = total
        for by in far_first:
            c, peer = col_peer(by)
            copy = send_to(result.at[own], result.at[own], s3.at[n, by], r3.at[n, gx - by], peer)
            copy.start()
            sent.append(copy)
        for by in range(1, gx):
            c, peer = col_peer(by)
            at = pl.ds(pl.multiple_of(c * rows, rows), rows)
            send_to(result.at[at], result.at[at], s3.at[n, by], r3.at[n, by], peer).wait_recv()
        for copy in sent:
            copy.wait_send()

    scale = 1.0 / total_rows
    all_reduce(0, inner_ref, one_in, piece, two_in, whole)
    proj = whole[...] * scale
    coef = jnp.concatenate(halves(proj), axis=0)
    step = 512
    gram = jnp.zeros((2 * rhs, 2 * rhs), F32)
    for i in range(0, columns, step):
        v = vbuf[:, :, i : i + step].reshape(blocks * rhs, step)
        out = dot(coef, v)
        resid = base_ref[:, i : i + step] - (out[:rhs] + out[rhs:])
        both = jnp.concatenate(halves(resid), axis=0)
        stack[:, i : i + step] = both
        gram = gram + dot(both, both, NT)
    gram_in[...] = gram[:rhs] + gram[rhs:]
    leaving = [
        pltpu.make_async_copy(stack, stack_ref, out_sem.at[0]),
        pltpu.make_async_copy(proj_buf, proj_ref, out_sem.at[1]),
    ]

    def hand_out():
        for i in range(0, blocks * rhs, 2 * rhs):
            proj_buf[i : i + 2 * rhs, :] = proj[:, i : i + 2 * rhs].T
        for copy in leaving:
            copy.start()

    all_reduce(1, gram_in, gone, narrow, two_gone, gram_out, hand_out)
    folded = gram_out[...] * scale
    folded = folded + pltpu.roll(folded, rhs, 1)
    lane = lax.broadcasted_iota(jnp.int32, (rhs, 2 * rhs), 1)
    row = lax.broadcasted_iota(jnp.int32, (rhs, 2 * rhs), 0)
    work = jnp.where(lane < rhs, folded, (lane - rhs == row).astype(F32))
    tall = 8
    count = rhs // tall
    part = [work[i * tall : (i + 1) * tall] for i in range(count)]
    low = lax.broadcasted_iota(jnp.int32, (tall, 2 * rhs), 0)
    for b in range(count):
        cols = [
            {i: jnp.broadcast_to(part[i][:, b * tall + t : b * tall + t + 1], (tall, 2 * rhs)) for i in range(b, count)}
            for t in range(tall)
        ]
        for t in range(tall):
            inverse = 1.0 / cols[t][b][t : t + 1, :]
            across = {u: cols[u][b][t : t + 1, :] * inverse for u in range(t + 1, tall)}
            pivot = part[b][t : t + 1, :] * inverse
            for i in range(b, count):
                factor = cols[t][i]
                if i == b:
                    factor = jnp.where(low > t, factor, 0.0)
                part[i] = part[i] - factor * pivot
                for u in range(t + 1, tall):
                    cols[u][i] = cols[u][i] - factor * across[u]
    work = jnp.concatenate(part, axis=0)
    diagonal = jnp.sum(jnp.where(lane == row, work, 0.0), axis=1, keepdims=True)
    work = work * lax.rsqrt(diagonal)
    factor_ref[...] = jnp.where((lane >= row) & (lane < rhs), work, 0.0).T[:rhs]
    right = jnp.where(lane < rhs, 0.0, work)
    right = right + pltpu.roll(right, rhs, 1)
    left_ref[...] = jnp.concatenate(halves(right), axis=0)
    for copy in leaving:
        copy.wait()
    for copy, arrival in crossings:
        copy.wait_send()
    for copy in started + list_sent:
        copy.wait_send()
    for copy in halo:
        copy.wait_send()


def step(basis, p2m, near_blocks, m2l, send_list, send_count, near_src, near_count, far_src, far_class):
    leaves, slots, panels, _ = near_blocks.shape
    blocks, rhs, columns = basis.shape
    classes, terms = m2l.shape[:2]
    peers = send_list.shape[1]
    units = 2 * leaves
    wide = blocks * rhs
    cuts = (0, 11, 20, units)
    depth = 4
    hbm = pl.BlockSpec(memory_space=pltpu.HBM)
    vmem = pl.BlockSpec(memory_space=pltpu.VMEM)
    smem = pl.BlockSpec(memory_space=pltpu.SMEM)
    dma = pltpu.SemaphoreType.DMA
    return pl.pallas_call(
        functools.partial(step_kernel, cuts, columns * peers),
        in_specs=[hbm, hbm, hbm, hbm, vmem, vmem, smem, smem, smem, smem],
        out_specs=(hbm, hbm, vmem, vmem),
        out_shape=(
            jax.ShapeDtypeStruct((2 * rhs, columns), BF16),
            jax.ShapeDtypeStruct((wide, rhs), F32),
            jax.ShapeDtypeStruct((2 * rhs, 2 * rhs), BF16),
            jax.ShapeDtypeStruct((rhs, rhs), F32),
        ),
        scratch_shapes=[
            pltpu.VMEM((wide, rhs), F32),
            dma((2,)),
            pltpu.VMEM((4, 2, 4, 4, units, rhs // 2, terms), BF16),
            pltpu.VMEM((3 * leaves, rhs, panels), BF16),
            pltpu.VMEM((depth, slots, panels, panels), BF16),
            pltpu.VMEM((leaves, panels, terms), BF16),
            pltpu.VMEM((units, rhs // 2, terms), BF16),
            pltpu.VMEM((8, peers), jnp.int32),
            pltpu.VMEM((4, 2, 4, 4, 8, peers), jnp.int32),
            pltpu.VMEM((rhs, columns), F32),
            pltpu.VMEM((blocks, rhs, columns), BF16),
            pltpu.VMEM((classes + 1, terms, terms), BF16),
            pltpu.VMEM((1, peers * 8), jnp.int32),
            pltpu.SMEM((1, peers * 8), jnp.int32),
            pltpu.VMEM((rhs, wide), F32),
            pltpu.VMEM((rhs, 2 * rhs), F32),
            pltpu.VMEM((8, 8, wide), F32),
            pltpu.VMEM((8, 8, wide), F32),
            pltpu.VMEM((2 * rhs, columns), BF16),
            pltpu.VMEM((2, 8, wide), F32),
            pltpu.VMEM((rhs, wide), F32),
            pltpu.VMEM((8, 8, 2 * rhs), F32),
            pltpu.VMEM((2, 8, 2 * rhs), F32),
            pltpu.VMEM((8, 8, 2 * rhs), F32),
            pltpu.VMEM((rhs, 2 * rhs), F32),
            dma((2, 8)), dma((2, 8)), dma((2, 8)), dma((2, 8)), dma((2, 8)), dma((2, 8)),
            dma, dma, dma,
            dma((3, 12, 4)), dma((3, 12, 4)), dma((3, 16)), dma((3, 16)),
            dma((2,)), dma((2,)), dma((4, 3)), dma((4, 3)),
            dma, dma, dma, dma, dma((depth,)),
        ],
        compiler_params=pltpu.CompilerParams(
            collective_id=0, has_side_effects=True, vmem_limit_bytes=LIMIT
        ),
        name="step",
    )(
        basis, p2m, near_blocks, m2l, jnp.swapaxes(send_list, 1, 2), send_count,
        near_src.T, near_count, far_src, far_class,
    )


def last_kernel(stack_ref, proj_in, left_ref, factor_in, next_ref, proj_ref, factor_ref):
    rhs = next_ref.shape[0]

    @pl.when(pl.program_id(0) == 0)
    def _():
        proj_ref[...] = proj_in[...]
        factor_ref[...] = factor_in[...]

    out = dot(left_ref[...], stack_ref[...])
    next_ref[...] = (out[:rhs] + out[rhs:]).astype(BF16)


def last(stack, proj, left, factor):
    double, columns = stack.shape
    rhs = double // 2
    steps = 2

    def fixed(array):
        return pl.BlockSpec(array.shape, lambda i: (0, 0))

    return pl.pallas_call(
        last_kernel,
        grid=(steps,),
        in_specs=[
            pl.BlockSpec((double, columns // steps), lambda i: (0, i)),
            fixed(proj), fixed(left), fixed(factor),
        ],
        out_specs=(
            pl.BlockSpec((rhs, columns // steps), lambda i: (0, i)), fixed(proj), fixed(factor),
        ),
        out_shape=(
            jax.ShapeDtypeStruct((rhs, columns), BF16),
            jax.ShapeDtypeStruct(proj.shape, F32),
            jax.ShapeDtypeStruct(factor.shape, F32),
        ),
        compiler_params=pltpu.CompilerParams(vmem_limit_bytes=LIMIT),
        name="last",
    )(stack, proj, left, factor)


def shards(
    basis, near_blocks, near_src, near_count, p2m, m2l, send_list, send_count, far_src, far_class
):
    blocks, rhs, columns = basis.shape
    stack, proj, left, factor = step(
        basis, p2m, near_blocks, m2l, send_list, send_count, near_src, near_count, far_src, far_class
    )
    new, proj, factor = last(stack, proj, left, factor)
    return (new, proj.reshape(blocks, rhs, rhs), factor)


def solution(mesh):
    finer = Mesh(mesh.devices.reshape(4, 2, 4, 4), ALL)
    in_specs = (
        P(None, None, ALL),
        P(ALL, None, None, None),
        P(ALL, None),
        P(ALL),
        P(ALL, None, None),
        P(),
        P(ALL, None, None),
        P(ALL, None),
        P(ALL, None),
        P(ALL, None),
    )
    out_specs = (P(None, ALL), P(), P())
    return jax.shard_map(
        shards, mesh=finer, in_specs=in_specs, out_specs=out_specs, check_vma=False
    )
```
